128 devices in a mesh: geom: 8 (over x, core), dom: 16 (over y, z).
Axes of the slice: x: 4, y: 4, z: 4, core: 2. Of those that a mesh axis runs over, the one named last changes fastest.
Arguments:
- h_in: bfloat16 [8, 8192, 512], P('geom', 'dom'), may hold values from -6 to 6
- edge_in: bfloat16 [8, 32768, 512], P('geom', 'dom'), may hold values from -6 to 6
- new_index: int32 [8, 8192], P('geom', 'dom'), may hold values from 0 to 8191, as said below
- source: int32 [8, 32768], P('geom', 'dom'), may hold values from 0 to 8191, as said below
- w_edge_in: bfloat16 [1536, 512], replicated, may hold values from -0.15625 to 0.15625
- w_edge_out: bfloat16 [512, 512], replicated, may hold values from -0.25 to 0.25
- w_node_in: bfloat16 [1024, 512], replicated, may hold values from -0.1875 to 0.1875
- w_node_out: bfloat16 [512, 512], replicated, may hold values from -0.25 to 0.25
- cot_nodes: bfloat16 [8, 8192, 512], P('geom', 'dom'), may hold values from -6 to 6
- cot_edges: bfloat16 [8, 32768, 512], P('geom', 'dom'), may hold values from -6 to 6
Outputs:
- node_new: bfloat16 [8, 8192, 512], P('geom', 'dom')
- edge_new: bfloat16 [8, 32768, 512], P('geom', 'dom')
- grad_in: bfloat16 [8, 8192, 512], P('geom', 'dom')
- grad_edge: bfloat16 [8, 32768, 512], P('geom', 'dom')
- weight_grads: float32 [3584, 512], P('dom')
The draws below stay inside these ranges and needn't reach their ends.
Inputs may be any that keep to these rules, and one draw needn't show every extreme that they name: `new_index`: per geometry a permutation of the 8192 cells. The cells in rows k * 512 to (k + 1) * 512 - 1 of the old layout reach the rows of any one device of the new layout at most 48 times, exactly 48 times for some pairs. `source`: an edge of a cell in rows k * 512 to (k + 1) * 512 - 1 comes from a cell of the same range, of the last 64 cells of the range before, or of the first 64 cells of the range after.
All inputs are finite; a program needn't handle non-finite values.
Results may differ from the reference program's by a relative error of at most 0.019.
Values may be sent and summed in bfloat16 or wider, within the bound.
A program may use at most 128 MiB of HBM per device.

```python
import math
import jax
import jax.numpy as jnp
import numpy as np
from jax import lax

D = 512
K = 4
C = 512
HB = 64
GEOMS = 8
PARTITIONS = 16
CELLS = 8192


def draw_new_index(key, part):
    base_count = C // PARTITIONS
    extra_count = base_count // 2
    counts = np.array([base_count + extra_count if offset % 2 == 0 else base_count - extra_count for offset in range(PARTITIONS)])
    bounds = jnp.asarray(np.cumsum(counts)[:-1], jnp.int32)

    def one_order(order_key):
        return jax.random.permutation(order_key, C).astype(jnp.int32)

    def one_geometry(geo_key):
        sub_keys = jax.random.split(geo_key, 2 * PARTITIONS)
        places = jax.vmap(one_order)(sub_keys[:PARTITIONS])
        shifts = jnp.sum((places[:, :, None] >= bounds[None, None, :]).astype(jnp.int32), axis=2)
        owners = (jnp.arange(PARTITIONS, dtype=jnp.int32)[:, None] + shifts) % PARTITIONS
        arrivals = jax.vmap(one_order)(sub_keys[PARTITIONS:])
        arrival_rows = arrivals[owners, places]
        return (owners * C + arrival_rows).reshape(-1).astype(jnp.int32)
    return jax.vmap(one_geometry)(jax.random.split(key, GEOMS))


def draw_source(key, part):

    def one_geometry(geo_key):
        sub_keys = jax.random.split(geo_key, 3)
        edge_ids = jnp.arange(CELLS * K, dtype=jnp.int32)
        cell_ids = edge_ids // K
        slot_ids = edge_ids % K
        device_ids = cell_ids // C
        row_ids = cell_ids % C
        kinds = jax.random.randint(sub_keys[0], (CELLS * K,), 0, 4, dtype=jnp.int32)
        local_pick = jax.random.randint(sub_keys[1], (CELLS * K,), 0, C, dtype=jnp.int32)
        rim_pick = jax.random.randint(sub_keys[2], (CELLS * K,), 0, HB, dtype=jnp.int32)
        from_prev = (kinds == 0) & (device_ids > 0) & (slot_ids > 0)
        from_next = (kinds == 1) & (device_ids < PARTITIONS - 1) & (slot_ids > 0)
        local_row = jnp.where(slot_ids == 0, (row_ids + 1) % C, local_pick)
        chosen = jnp.where(from_prev, (device_ids - 1) * C + C - HB + rim_pick, jnp.where(from_next, (device_ids + 1) * C + rim_pick, device_ids * C + local_row))
        return chosen.astype(jnp.int32)
    return jax.vmap(one_geometry)(jax.random.split(key, GEOMS))


def shard_levels(rng, dims, cuts, smallest, top_value):
    def one(axis_at, blocks):
        draws = jax.random.uniform(jax.random.fold_in(jax.random.fold_in(rng, 6), axis_at), (blocks,), jnp.float32, smallest / len(cuts), top_value / len(cuts))
        return jnp.repeat(jnp.exp(draws), dims[axis_at] // blocks).reshape((-1,) + (1,) * (len(dims) - axis_at - 1))

    loudness = one(*cuts[0])
    for cut in cuts[1:]:
        loudness = loudness * one(*cut)
    return loudness


def normal_values(own_key, dims, deviation, limit, pieces=(), kind=jnp.bfloat16):
    entries = jax.random.normal(own_key, dims, jnp.float32) * deviation
    if len(pieces) > 0:
        entries = shard_levels(own_key, dims, pieces, -0.22, 0.18) * entries
    return jnp.clip(entries, min=-limit, max=limit).astype(kind)


def setup_inputs(seed: int = 0) -> dict:
    key_of = jax.random.split(jax.random.key(seed), 11)
    return {
        "h_in": normal_values(key_of[0], (GEOMS, CELLS, D), 1.0, 6.0, ((0, 8), (1, 16))),
        "edge_in": normal_values(key_of[1], (GEOMS, CELLS * K, D), 1.0, 6.0, ((0, 8), (1, 16))),
        "new_index": draw_new_index(jax.random.fold_in(key_of[10], 71), 0),
        "source": draw_source(jax.random.fold_in(key_of[10], 71), 0),
        "w_edge_in": normal_values(key_of[4], (3 * D, D), (3 * D) ** -0.5, 0.15625),
        "w_edge_out": normal_values(key_of[5], (D, D), D ** -0.5, 0.25),
        "w_node_in": normal_values(key_of[6], (2 * D, D), (2 * D) ** -0.5, 0.1875),
        "w_node_out": normal_values(key_of[7], (D, D), D ** -0.5, 0.25),
        "cot_nodes": normal_values(key_of[8], (GEOMS, CELLS, D), 1.0, 6.0, ((0, 8), (1, 16))),
        "cot_edges": normal_values(key_of[9], (GEOMS, CELLS * K, D), 1.0, 6.0, ((0, 8), (1, 16))),
    }


def normalize(values):
    center = values - lax.optimization_barrier(jnp.mean(values, axis=-1, keepdims=True))
    inverse = lax.rsqrt(lax.optimization_barrier(jnp.mean(center * center, axis=-1, keepdims=True)) + 1e-05)
    return (center * inverse, inverse)

def normalize_back(normed, inverse, upstream):
    return inverse * (upstream - lax.optimization_barrier(jnp.mean(upstream, axis=-1, keepdims=True)) - normed * lax.optimization_barrier(jnp.mean(upstream * normed, axis=-1, keepdims=True)))

def silu_slope(values):
    sigma = jax.nn.sigmoid(values)
    return sigma * (1.0 + values * (1.0 - sigma))

def matmul(left, right):
    return jnp.dot(left, right, preferred_element_type=jnp.float32)

def layer_math(nodes, edges, senders, w_edge_in, w_edge_out, w_node_in, w_node_out, cot_nodes, cot_edges, fan_in):
    width = nodes.shape[1]
    cell_count = nodes.shape[0]
    receivers = jnp.repeat(nodes, fan_in, axis=0)
    w_edge_self = w_edge_in[:width]
    w_edge_send = w_edge_in[width:2 * width]
    w_edge_recv = w_edge_in[2 * width:]
    w_node_self = w_node_in[:width]
    w_node_agg = w_node_in[width:]
    edge_pre = matmul(edges, w_edge_self) + matmul(senders, w_edge_send) + matmul(receivers, w_edge_recv)
    edge_hidden = jax.nn.silu(edge_pre).astype(jnp.bfloat16)
    edge_post = matmul(edge_hidden, w_edge_out)
    edge_normed, edge_inverse = normalize(edge_post)
    edge_new = (edges.astype(jnp.float32) + edge_normed).astype(jnp.bfloat16)
    summed = lax.optimization_barrier(jnp.sum(edge_new.astype(jnp.float32).reshape(cell_count, fan_in, width), axis=1)).astype(jnp.bfloat16)
    node_pre = matmul(nodes, w_node_self) + matmul(summed, w_node_agg)
    node_hidden = jax.nn.silu(node_pre).astype(jnp.bfloat16)
    node_post = matmul(node_hidden, w_node_out)
    node_normed, node_inverse = normalize(node_post)
    node_new = (nodes.astype(jnp.float32) + node_normed).astype(jnp.bfloat16)
    node_upstream = cot_nodes.astype(jnp.float32)
    node_post_grad = normalize_back(node_normed, node_inverse, node_upstream).astype(jnp.bfloat16)
    grad_node_out = matmul(node_hidden.T, node_post_grad)
    node_pre_grad = (matmul(node_post_grad, w_node_out.T) * silu_slope(node_pre)).astype(jnp.bfloat16)
    grad_node_self = matmul(nodes.T, node_pre_grad)
    grad_node_agg = matmul(summed.T, node_pre_grad)
    summed_grad = matmul(node_pre_grad, w_node_agg.T)
    edge_upstream = cot_edges.astype(jnp.float32) + jnp.repeat(summed_grad, fan_in, axis=0)
    edge_post_grad = normalize_back(edge_normed, edge_inverse, edge_upstream).astype(jnp.bfloat16)
    grad_edge_out = matmul(edge_hidden.T, edge_post_grad)
    edge_pre_grad = (matmul(edge_post_grad, w_edge_out.T) * silu_slope(edge_pre)).astype(jnp.bfloat16)
    grad_edge_self = matmul(edges.T, edge_pre_grad)
    grad_edge_send = matmul(senders.T, edge_pre_grad)
    grad_edge_recv = matmul(receivers.T, edge_pre_grad)
    grad_edge = (edge_upstream + matmul(edge_pre_grad, w_edge_self.T)).astype(jnp.bfloat16)
    sender_grad = matmul(edge_pre_grad, w_edge_send.T)
    receiver_grad = lax.optimization_barrier(jnp.sum(matmul(edge_pre_grad, w_edge_recv.T).reshape(cell_count, fan_in, width), axis=1))
    node_grad = node_upstream + matmul(node_pre_grad, w_node_self.T) + receiver_grad
    stacked = jnp.concatenate([grad_edge_self, grad_edge_send, grad_edge_recv, grad_edge_out, grad_node_self, grad_node_agg, grad_node_out], axis=0)
    return (node_new, edge_new, grad_edge, node_grad, sender_grad, stacked)

def reference(h_in, edge_in, new_index, source, w_edge_in, w_edge_out, w_node_in, w_node_out, cot_nodes, cot_edges):
    node_list = []
    edge_list = []
    grad_in_list = []
    grad_edge_list = []
    total = jnp.zeros((7 * D, D), jnp.float32)
    for geometry in range(GEOMS):
        places = new_index[geometry].astype(jnp.int32)
        senders_at = source[geometry].astype(jnp.int32)
        nodes = jnp.zeros((CELLS, D), jnp.bfloat16).at[places].set(h_in[geometry])
        senders = nodes[senders_at]
        node_new, edge_new, grad_edge, node_grad, sender_grad, stacked = layer_math(nodes, edge_in[geometry], senders, w_edge_in, w_edge_out, w_node_in, w_node_out, cot_nodes[geometry], cot_edges[geometry], K)
        node_grad = node_grad + jnp.zeros((CELLS, D), jnp.float32).at[senders_at].add(sender_grad)
        grad_in_list.append(node_grad.astype(jnp.bfloat16)[places])
        node_list.append(node_new)
        edge_list.append(edge_new)
        grad_edge_list.append(grad_edge)
        total = total + stacked
    weight_grads = total * (1.0 / math.sqrt(GEOMS * CELLS * K))
    return (jnp.stack(node_list), jnp.stack(edge_list), jnp.stack(grad_in_list), jnp.stack(grad_edge_list), weight_grads)
```

```python
import functools
import math

import jax
import jax.numpy as jnp
from jax import lax
from jax.experimental import pallas as pl
from jax.experimental.pallas import tpu as pltpu
from jax.sharding import PartitionSpec as P

MESH = pl.DeviceIdType.MESH
BF = jnp.bfloat16
F32 = jnp.float32

D = 512
K = 4
C = 512
HB = 64
PADDED = C + 2 * HB
NP = 16
CAP = 48
SLOTS = NP * CAP
TC = 128
TE = TC * K
TILES = C // TC
SEL = PADDED + TC
RC = 64
SQUARES = 7
PER_DOM = SQUARES * D // NP
PER_CORE = PER_DOM // 2


def nn(a, b):
    return jnp.dot(a, b, preferred_element_type=F32)


def nt(a, b):
    return lax.dot_general(a, b, (((1,), (1,)), ((), ())), preferred_element_type=F32)


def tn(a, b):
    return lax.dot_general(a, b, (((0,), (0,)), ((), ())), preferred_element_type=F32)


def sigmoid(v):
    return 0.5 * jnp.tanh(0.5 * v) + 0.5


def iota(shape, dim):
    return lax.broadcasted_iota(jnp.int32, shape, dim)


def remote(src, dst, send, recv, geom, dom):
    return pltpu.make_async_remote_copy(
        src_ref=src,
        dst_ref=dst,
        send_sem=send,
        recv_sem=recv,
        device_id=(geom, dom),
        device_id_type=MESH,
    )


def signal(sem, geom, dom):
    pl.semaphore_signal(sem, inc=1, device_id=(geom, dom), device_id_type=MESH)


def pack_matrix(slot):
    return (iota((SLOTS, C), 0) == slot).astype(BF)


def unpack_blocks(ids):
    turned = ids.T
    lanes = iota((CAP, C), 1).astype(F32)
    return [(turned[0:CAP, p : p + 1] == lanes).astype(BF) for p in range(NP)]


def deliver_kernel(
    h_ref, tgt_ref, pad_ref, ids_ref, slot_ref,
    sbuf, rbuf, sids, rids, edge_out, edge_in, mt,
    send, recv, isend, irecv, hsend, hrecv,
):
    geom = lax.axis_index("geom")
    me = lax.axis_index("dom")
    barrier = pltpu.get_barrier_semaphore()
    for p in range(1, NP):
        signal(barrier, geom, (me + p) % NP)

    tgt = tgt_ref[...]
    off = ((tgt >> 9) - me) & (NP - 1)
    row = tgt & (C - 1)
    owned = (iota((NP, C), 0) == off).astype(F32)
    upper = (iota((C, C), 0) < iota((C, C), 1)).astype(BF)
    before = nn(owned.astype(BF), upper)
    rank = jnp.sum(owned * before, axis=0, keepdims=True).astype(jnp.int32)
    slot = off * CAP + rank
    slot_ref[...] = slot
    ranked = (iota((128, C), 0) == rank).astype(BF)
    high = (row >> 5).astype(F32)
    low = (row & 31).astype(F32)
    coded = nt(jnp.concatenate([owned * high, owned * low, owned], axis=0).astype(BF), ranked)
    ids = 32.0 * coded[0:NP] + coded[NP : 2 * NP] + coded[2 * NP :] - 1.0
    for p in range(NP):
        sids[p] = jnp.broadcast_to(ids[p : p + 1, :], (8, 128))
    packed = nn(pack_matrix(slot), h_ref[...]).astype(BF)
    sbuf[...] = packed.reshape(NP, CAP, D)
    rbuf[0] = packed[0:CAP]

    pl.semaphore_wait(barrier, NP - 1)
    copies = []
    for p in range(1, NP):
        peer = (me + p) % NP
        copies.append(remote(sids.at[p], rids.at[p], isend.at[p], irecv.at[p], geom, peer))
        copies.append(remote(sbuf.at[p], rbuf.at[p], send.at[p], recv.at[p], geom, peer))
    for copy in copies:
        copy.start()
    for copy in copies[0::2]:
        copy.wait_recv()
    got = jnp.concatenate([ids[0:1]] + [rids[p, 0:1, :] for p in range(1, NP)], axis=0)
    ids_ref[...] = got
    for p, block in enumerate(unpack_blocks(got)):
        mt[pl.ds(p * CAP, CAP), :] = block
    for copy in copies[1::2]:
        copy.wait_recv()
    nodes = tn(mt[...], rbuf[...].reshape(SLOTS, D)).astype(BF)
    edge_out[0] = nodes[0:HB]
    edge_out[1] = nodes[C - HB : C]
    to_prev = remote(edge_out.at[0], edge_in.at[1], hsend.at[0], hrecv.at[1], geom, (me + NP - 1) % NP)
    to_next = remote(edge_out.at[1], edge_in.at[0], hsend.at[1], hrecv.at[0], geom, (me + 1) % NP)
    to_prev.start()
    to_next.start()
    pad_ref[HB : HB + C, :] = nodes
    to_prev.wait_recv()
    to_next.wait_recv()
    pad_ref[0:HB, :] = edge_in[0]
    pad_ref[HB + C :, :] = edge_in[1]
    for copy in copies:
        copy.wait_send()
    to_prev.wait_send()
    to_next.wait_send()


def deliver(h, tgt):
    vm = pl.BlockSpec(memory_space=pltpu.VMEM)
    return pl.pallas_call(
        deliver_kernel,
        out_shape=(
            jax.ShapeDtypeStruct((PADDED, D), BF),
            jax.ShapeDtypeStruct((NP, 128), F32),
            jax.ShapeDtypeStruct((1, C), jnp.int32),
        ),
        in_specs=[vm, vm],
        out_specs=(vm, vm, vm),
        scratch_shapes=[
            pltpu.VMEM((NP, CAP, D), BF),
            pltpu.VMEM((NP, CAP, D), BF),
            pltpu.VMEM((NP, 8, 128), F32),
            pltpu.VMEM((NP, 8, 128), F32),
            pltpu.VMEM((2, HB, D), BF),
            pltpu.VMEM((2, HB, D), BF),
            pltpu.VMEM((SLOTS, C), BF),
        ]
        + [pltpu.SemaphoreType.DMA((NP,))] * 4
        + [pltpu.SemaphoreType.DMA((2,))] * 2,
        compiler_params=pltpu.CompilerParams(collective_id=0, has_side_effects=True),
        name="deliver",
    )(h, tgt)


def layer_kernel(
    pad_ref, src_ref, edges_ref, cotn_ref, cote_ref, wei_ref, weo_ref, wni_ref, wno_ref,
    edge_new_ref, node_new_ref, grad_edge_ref, ng_ref, halo_ref, w_ref,
    sel, sel_t, comb, spread, gather4,
    big, slope, hid, normed, inv, ups, post_grad, pre_grad,
    total, acc,
):
    step = pl.program_id(0)
    me = lax.axis_index("dom")
    w_self, w_send, w_recv = wei_ref.at[0:D], wei_ref.at[D : 2 * D], wei_ref.at[2 * D : 3 * D]
    w_nself, w_nagg = wni_ref.at[0:D], wni_ref.at[D : 2 * D]
    rows = pl.ds(pl.multiple_of(step * TC, TC), TC)

    @pl.when(step == 0)
    def _():
        comb[0:PADDED, :] = nn(pad_ref[...], w_send[...]).astype(BF)
        sel[:, PADDED:] = (iota((TE, TC), 0) // K == iota((TE, TC), 1)).astype(BF)
        sel_t[PADDED:, :] = (iota((TC, TE), 1) // K == iota((TC, TE), 0)).astype(BF)
        total[...] = jnp.zeros_like(total)
        acc[...] = jnp.zeros_like(acc)

    nodes = pad_ref[pl.ds(pl.multiple_of(HB + step * TC, HB), TC), :]
    edges = edges_ref[...]
    src = src_ref[...] - (me * C - HB)
    sel_t[0:PADDED, :] = (iota((PADDED, TE), 0) == src).astype(BF)
    src_col = jnp.broadcast_to(src.astype(F32), (128, TE)).T.astype(jnp.int32)
    for b in range(PADDED // 128):
        sel[:, b * 128 : (b + 1) * 128] = (src_col == iota((TE, 128), 1) + b * 128).astype(BF)
    comb[PADDED:, :] = nn(nodes, w_recv[...]).astype(BF)

    big[...] = nn(edges, w_self[...]) + nn(sel[...], comb[...])
    for r in range(0, TE, RC):
        v = big[r : r + RC, :]
        s = sigmoid(v)
        h = v * s
        hid[r : r + RC, :] = h.astype(BF)
        slope[r : r + RC, :] = s + h * (1.0 - s)
    big[...] = nn(hid[...], weo_ref[...])
    for r in range(0, TE, RC):
        v = big[r : r + RC, :]
        center = v - jnp.mean(v, axis=-1, keepdims=True)
        i = lax.rsqrt(jnp.mean(center * center, axis=-1, keepdims=True) + 1e-05)
        n = center * i
        normed[r : r + RC, :] = n
        inv[r : r + RC, :] = jnp.broadcast_to(i, (RC, 128))
        edge_new_ref[r : r + RC, :] = (edges_ref[r : r + RC, :].astype(F32) + n).astype(BF)

    four = sel_t[PADDED:, :]
    summed = nn(four, edge_new_ref[...]).astype(BF)
    v = nn(nodes, w_nself[...]) + nn(summed, w_nagg[...])
    s = sigmoid(v)
    h = v * s
    node_slope = s + h * (1.0 - s)
    node_hid = h.astype(BF)
    v = nn(node_hid, wno_ref[...])
    center = v - jnp.mean(v, axis=-1, keepdims=True)
    i = lax.rsqrt(jnp.mean(center * center, axis=-1, keepdims=True) + 1e-05)
    n = center * i
    node_new_ref[...] = (nodes.astype(F32) + n).astype(BF)
    u = cotn_ref[...].astype(F32)
    m1 = jnp.mean(u, axis=-1, keepdims=True)
    m2 = jnp.mean(u * n, axis=-1, keepdims=True)
    node_post_grad = (i * (u - m1 - n * m2)).astype(BF)
    node_pre_grad = (nt(node_post_grad, wno_ref[...]) * node_slope).astype(BF)
    spread_grad = nt(node_pre_grad, w_nagg[...]).astype(BF)

    ups[...] = nn(sel[:, PADDED:], spread_grad)
    for r in range(0, TE, RC):
        u = cote_ref[r : r + RC, :].astype(F32) + ups[r : r + RC, :]
        ups[r : r + RC, :] = u
        n = normed[r : r + RC, :]
        m1 = jnp.mean(u, axis=-1, keepdims=True)
        m2 = jnp.mean(u * n, axis=-1, keepdims=True)
        post_grad[r : r + RC, :] = (inv[r : r + RC, 0:1] * (u - m1 - n * m2)).astype(BF)
    big[...] = nt(post_grad[...], weo_ref[...])
    for r in range(0, TE, RC):
        pre_grad[r : r + RC, :] = (big[r : r + RC, :] * slope[r : r + RC, :]).astype(BF)
    g = pre_grad[...]
    big[...] = nt(g, w_self[...])
    for r in range(0, TE, RC):
        grad_edge_ref[r : r + RC, :] = (ups[r : r + RC, :] + big[r : r + RC, :]).astype(BF)
    total[...] += nn(sel_t[0:PADDED, :], g)
    recv_grad = nn(four, g).astype(BF)
    ng_ref[rows, :] = (
        cotn_ref[...].astype(F32) + nt(node_pre_grad, w_nself[...]) + nt(recv_grad, w_recv[...])
    )
    acc[0:D, :] += tn(edges, g)
    acc[2 * D : 3 * D, :] += tn(nodes, recv_grad)
    acc[3 * D : 4 * D, :] += tn(hid[...], post_grad[...])
    acc[4 * D : 5 * D, :] += tn(nodes, node_pre_grad)
    acc[5 * D : 6 * D, :] += tn(summed, node_pre_grad)
    acc[6 * D : 7 * D, :] += tn(node_hid, node_post_grad)

    @pl.when(step == TILES - 1)
    def _():
        scale = 1.0 / math.sqrt(8 * NP * C * K)
        t = total[...].astype(BF)
        acc[D : 2 * D, :] = tn(pad_ref[...], t)
        back = nt(t, w_send[...])
        ng_ref[...] += back[HB : HB + C]
        halo_ref[0] = back[0:HB].astype(BF)
        halo_ref[1] = back[HB + C :].astype(BF)
        w_ref[...] = (acc[...] * scale).astype(BF)


def layer(padded, source, edges, cot_nodes, cot_edges, wei, weo, wni, wno):
    def whole(shape):
        return pl.BlockSpec(shape, lambda i: (0,) * len(shape), pipeline_mode=pl.Buffered(1))

    def tile(rows):
        return pl.BlockSpec((rows, D), lambda i: (i, 0))

    return pl.pallas_call(
        layer_kernel,
        grid=(TILES,),
        out_shape=(
            jax.ShapeDtypeStruct((C * K, D), BF),
            jax.ShapeDtypeStruct((C, D), BF),
            jax.ShapeDtypeStruct((C * K, D), BF),
            jax.ShapeDtypeStruct((C, D), F32),
            jax.ShapeDtypeStruct((2, HB, D), BF),
            jax.ShapeDtypeStruct((SQUARES * D, D), BF),
        ),
        in_specs=[
            whole((PADDED, D)),
            pl.BlockSpec((1, TE), lambda i: (0, i)),
            tile(TE),
            tile(TC),
            tile(TE),
            whole((3 * D, D)),
            whole((D, D)),
            whole((2 * D, D)),
            whole((D, D)),
        ],
        out_specs=(
            tile(TE),
            tile(TC),
            tile(TE),
            whole((C, D)),
            whole((2, HB, D)),
            whole((SQUARES * D, D)),
        ),
        scratch_shapes=[
            pltpu.VMEM((TE, SEL), BF),
            pltpu.VMEM((SEL, TE), BF),
            pltpu.VMEM((SEL, D), BF),
            pltpu.VMEM((8, 128), BF),
            pltpu.VMEM((8, 128), BF),
            pltpu.VMEM((TE, D), F32),
            pltpu.VMEM((TE, D), F32),
            pltpu.VMEM((TE, D), BF),
            pltpu.VMEM((TE, D), F32),
            pltpu.VMEM((TE, 128), F32),
            pltpu.VMEM((TE, D), F32),
            pltpu.VMEM((TE, D), BF),
            pltpu.VMEM((TE, D), BF),
            pltpu.VMEM((PADDED, D), F32),
            pltpu.VMEM((SQUARES * D, D), F32),
        ],
        compiler_params=pltpu.CompilerParams(vmem_limit_bytes=60 * 1024 * 1024),
        name="layer",
    )(padded, source, edges, cot_nodes, cot_edges, wei, weo, wni, wno)


def collect_kernel(
    ng_ref, halo_ref, w_ref, ids_ref, slot_ref, grad_ref, out_ref,
    hbuf, sback, rback, pbuf, wsum, r1a, r1b, p1a, p1b, r2a, r2b, r3, fin,
    hsend, hrecv, bsend, brecv, psend, precv, s1a, v1a, s1b, v1b,
    s2a, v2a, s2b, v2b, s3, v3, s4, v4,
):
    geom = lax.axis_index("geom")
    me = lax.axis_index("dom")
    core = geom % 2
    x = geom // 2
    y = me // 4
    z = me % 4
    partner = x * 2 + (1 - core)
    barrier = pltpu.get_barrier_semaphore()
    signal(barrier, partner, me)
    for p in range(1, NP):
        signal(barrier, geom, (me + p) % NP)
    for d in range(1, 4):
        signal(barrier, ((x + d) % 4) * 2 + core, me)
    pl.semaphore_wait(barrier, NP + 3)

    to_prev = remote(halo_ref.at[0], hbuf.at[1], hsend.at[0], hrecv.at[1], geom, (me + NP - 1) % NP)
    to_next = remote(halo_ref.at[1], hbuf.at[0], hsend.at[1], hrecv.at[0], geom, (me + 1) % NP)
    to_prev.start()
    to_next.start()
    pair = [
        remote(w_ref.at[i, :, 1 - core], pbuf.at[i], psend.at[i], precv.at[i], partner, me)
        for i in range(4)
    ]
    for copy in pair:
        copy.start()

    blocks = unpack_blocks(ids_ref[...])
    to_prev.wait_recv()
    to_next.wait_recv()
    first = ng_ref[0:HB, :] + hbuf[0].astype(F32)
    last = ng_ref[C - HB :, :] + hbuf[1].astype(F32)
    cells = jnp.concatenate([first, ng_ref[HB : C - HB, :], last], axis=0).astype(BF)
    packed = nn(jnp.concatenate(blocks, axis=0), cells).astype(BF)
    sback[...] = packed.reshape(NP, CAP, D)
    rback[0] = packed[0:CAP]
    backs = [
        remote(sback.at[p], rback.at[p], bsend.at[p], brecv.at[p], geom, (me + NP - p) % NP)
        for p in range(1, NP)
    ]
    for copy in backs:
        copy.start()

    for i in range(4):
        pair[i].wait_recv()
        for j in range(4):
            mine = w_ref[i, j, pl.ds(core, 1)].reshape(PER_CORE, D)
            wsum[i, j] = (mine.astype(F32) + pbuf[i, j].astype(F32)).astype(BF)

    half = D // 2
    ones = []
    for d in range(1, 4):
        ty, tz = (y + d) % 4, (z + d) % 4
        ones.append(
            remote(wsum.at[ty, :, :, 0:half], r1a.at[d - 1], s1a.at[d - 1], v1a.at[d - 1], geom, ty * 4 + z)
        )
        ones.append(
            remote(wsum.at[:, tz, :, half:D], r1b.at[d - 1], s1b.at[d - 1], v1b.at[d - 1], geom, y * 4 + tz)
        )
    for copy in ones:
        copy.start()

    for copy in backs:
        copy.wait_recv()
    grad_ref[...] = tn(pack_matrix(slot_ref[...]), rback[...].reshape(SLOTS, D)).astype(BF)

    for copy in ones:
        copy.wait_recv()
    for j in range(4):
        own = wsum[pl.ds(y, 1), j, :, 0:half].reshape(PER_CORE, half).astype(F32)
        for d in range(3):
            own += r1a[d, j].astype(F32)
        p1a[j] = own.astype(BF)
        own = wsum[j, pl.ds(z, 1), :, half:D].reshape(PER_CORE, half).astype(F32)
        for d in range(3):
            own += r1b[d, j].astype(F32)
        p1b[j] = own.astype(BF)
    twos = []
    for d in range(1, 4):
        ty, tz = (y + d) % 4, (z + d) % 4
        twos.append(remote(p1a.at[tz], r2a.at[d - 1], s2a.at[d - 1], v2a.at[d - 1], geom, y * 4 + tz))
        twos.append(remote(p1b.at[ty], r2b.at[d - 1], s2b.at[d - 1], v2b.at[d - 1], geom, ty * 4 + z))
    for copy in twos:
        copy.start()
    for copy in twos:
        copy.wait_recv()
    left = p1a[pl.ds(z, 1)].reshape(PER_CORE, half).astype(F32)
    right = p1b[pl.ds(y, 1)].reshape(PER_CORE, half).astype(F32)
    for d in range(3):
        left += r2a[d].astype(F32)
        right += r2b[d].astype(F32)
    r3[pl.ds(x, 1)] = jnp.concatenate([left, right], axis=1).astype(BF).reshape(1, PER_CORE, D)
    threes = [
        remote(r3.at[x], r3.at[x], s3.at[d - 1], v3.at[d - 1], ((x + d) % 4) * 2 + core, me)
        for d in range(1, 4)
    ]
    for copy in threes:
        copy.start()
    for d in range(1, 4):
        source = (x + 4 - d) % 4
        remote(r3.at[x], r3.at[source], s3.at[d - 1], v3.at[d - 1], source * 2 + core, me).wait_recv()
    done = r3[0].astype(F32) + r3[1].astype(F32) + r3[2].astype(F32) + r3[3].astype(F32)
    fin[pl.ds(core, 1)] = done.reshape(1, PER_CORE, D)
    four = remote(fin.at[core], fin.at[core], s4, v4, partner, me)
    four.start()
    remote(fin.at[core], fin.at[1 - core], s4, v4, partner, me).wait_recv()
    out_ref[...] = fin[...].reshape(PER_DOM, D)
    for copy in [to_prev, to_next] + pair + backs + ones + twos + threes + [four]:
        copy.wait_send()


def collect(ng, halo, w, ids, slot):
    vm = pl.BlockSpec(memory_space=pltpu.VMEM)
    half = D // 2
    dma = pltpu.SemaphoreType.DMA
    return pl.pallas_call(
        collect_kernel,
        out_shape=(
            jax.ShapeDtypeStruct((C, D), BF),
            jax.ShapeDtypeStruct((PER_DOM, D), F32),
        ),
        in_specs=[vm] * 5,
        out_specs=(vm, vm),
        scratch_shapes=[
            pltpu.VMEM((2, HB, D), BF),
            pltpu.VMEM((NP, CAP, D), BF),
            pltpu.VMEM((NP, CAP, D), BF),
            pltpu.VMEM((4, 4, PER_CORE, D), BF),
            pltpu.VMEM((4, 4, PER_CORE, D), BF),
            pltpu.VMEM((3, 4, PER_CORE, half), BF),
            pltpu.VMEM((3, 4, PER_CORE, half), BF),
            pltpu.VMEM((4, PER_CORE, half), BF),
            pltpu.VMEM((4, PER_CORE, half), BF),
            pltpu.VMEM((3, PER_CORE, half), BF),
            pltpu.VMEM((3, PER_CORE, half), BF),
            pltpu.VMEM((4, PER_CORE, D), BF),
            pltpu.VMEM((2, PER_CORE, D), F32),
            dma((2,)), dma((2,)), dma((NP,)), dma((NP,)), dma((4,)), dma((4,)),
            dma((3,)), dma((3,)), dma((3,)), dma((3,)),
            dma((3,)), dma((3,)), dma((3,)), dma((3,)),
            dma((3,)), dma((3,)), dma, dma,
        ],
        compiler_params=pltpu.CompilerParams(collective_id=1, has_side_effects=True),
        name="collect",
    )(ng, halo, w, ids, slot)


def local(
    h_in, edge_in, new_index, source, w_edge_in, w_edge_out, w_node_in, w_node_out, cot_nodes, cot_edges
):
    padded, ids, slot = deliver(h_in[0], new_index)
    edge_new, node_new, grad_edge, ng, halo, w = layer(
        padded, source, edge_in[0], cot_nodes[0], cot_edges[0], w_edge_in, w_edge_out, w_node_in, w_node_out
    )
    grad_in, weight_grads = collect(ng, halo, w.reshape(4, 4, 2, PER_CORE, D), ids, slot)
    return (node_new[None], edge_new[None], grad_in[None], grad_edge[None], weight_grads)


def solution(mesh):
    return jax.shard_map(
        local,
        mesh=mesh,
        in_specs=(
            P("geom", "dom", None),
            P("geom", "dom", None),
            P("geom", "dom"),
            P("geom", "dom"),
            P(),
            P(),
            P(),
            P(),
            P("geom", "dom", None),
            P("geom", "dom", None),
        ),
        out_specs=(
            P("geom", "dom", None),
            P("geom", "dom", None),
            P("geom", "dom", None),
            P("geom", "dom", None),
            P("dom", None),
        ),
        check_vma=False,
    )
```

```python
import functools
import math

import jax
import jax.numpy as jnp
from jax import lax
from jax.experimental import pallas as pl
from jax.experimental.pallas import tpu as pltpu
from jax.sharding import PartitionSpec as P

MESH = pl.DeviceIdType.MESH
BF = jnp.bfloat16
F32 = jnp.float32

D = 512
K = 4
C = 512
HB = 64
PADDED = C + 2 * HB
NP = 16
CAP = 48
SLOTS = NP * CAP
TC = 128
TE = TC * K
TILES = C // TC
SEL = PADDED + TC
RC = 64
SQUARES = 7
PER_DOM = SQUARES * D // NP


def nn(a, b):
    return jnp.dot(a, b, preferred_element_type=F32)


def nt(a, b):
    return lax.dot_general(a, b, (((1,), (1,)), ((), ())), preferred_element_type=F32)


def tn(a, b):
    return lax.dot_general(a, b, (((0,), (0,)), ((), ())), preferred_element_type=F32)


def sigmoid(v):
    return 0.5 * jnp.tanh(0.5 * v) + 0.5


def iota(shape, dim):
    return lax.broadcasted_iota(jnp.int32, shape, dim)


def remote(src, dst, send, recv, geom, dom):
    return pltpu.make_async_remote_copy(
        src_ref=src,
        dst_ref=dst,
        send_sem=send,
        recv_sem=recv,
        device_id=(geom, dom),
        device_id_type=MESH,
    )


def signal(sem, geom, dom):
    pl.semaphore_signal(sem, inc=1, device_id=(geom, dom), device_id_type=MESH)


def pack_matrix(slot):
    return (iota((SLOTS, C), 0) == slot).astype(BF)


def unpack_blocks(ids):
    turned = ids.T
    lanes = iota((CAP, C), 1).astype(F32)
    return [(turned[0:CAP, p : p + 1] == lanes).astype(BF) for p in range(NP)]


def deliver_kernel(
    h_ref, tgt_ref, pad_ref, ids_ref, slot_ref,
    sbuf, rbuf, sids, rids, edge_out, edge_in, mt,
    send, recv, isend, irecv, hsend, hrecv,
):
    geom = lax.axis_index("geom")
    me = lax.axis_index("dom")
    barrier = pltpu.get_barrier_semaphore()
    for p in range(1, NP):
        signal(barrier, geom, (me + p) % NP)

    tgt = tgt_ref[...]
    off = ((tgt >> 9) - me) & (NP - 1)
    row = tgt & (C - 1)
    owned = (iota((NP, C), 0) == off).astype(F32)
    upper = (iota((C, C), 0) < iota((C, C), 1)).astype(BF)
    before = nn(owned.astype(BF), upper)
    rank = jnp.sum(owned * before, axis=0, keepdims=True).astype(jnp.int32)
    slot = off * CAP + rank
    slot_ref[...] = slot
    ranked = (iota((128, C), 0) == rank).astype(BF)
    high = (row >> 5).astype(F32)
    low = (row & 31).astype(F32)
    coded = nt(jnp.concatenate([owned * high, owned * low, owned], axis=0).astype(BF), ranked)
    ids = 32.0 * coded[0:NP] + coded[NP : 2 * NP] + coded[2 * NP :] - 1.0
    for p in range(NP):
        sids[p] = jnp.broadcast_to(ids[p : p + 1, :], (8, 128))
    packed = nn(pack_matrix(slot), h_ref[...]).astype(BF)
    sbuf[...] = packed.reshape(NP, CAP, D)
    rbuf[0] = packed[0:CAP]

    pl.semaphore_wait(barrier, NP - 1)
    copies = []
    for p in range(1, NP):
        peer = (me + p) % NP
        copies.append(remote(sids.at[p], rids.at[p], isend.at[p], irecv.at[p], geom, peer))
        copies.append(remote(sbuf.at[p], rbuf.at[p], send.at[p], recv.at[p], geom, peer))
    for copy in copies:
        copy.start()
    for copy in copies[0::2]:
        copy.wait_recv()
    got = jnp.concatenate([ids[0:1]] + [rids[p, 0:1, :] for p in range(1, NP)], axis=0)
    ids_ref[...] = got
    for p, block in enumerate(unpack_blocks(got)):
        mt[pl.ds(p * CAP, CAP), :] = block
    for copy in copies[1::2]:
        copy.wait_recv()
    nodes = tn(mt[...], rbuf[...].reshape(SLOTS, D)).astype(BF)
    edge_out[0] = nodes[0:HB]
    edge_out[1] = nodes[C - HB : C]
    to_prev = remote(edge_out.at[0], edge_in.at[1], hsend.at[0], hrecv.at[1], geom, (me + NP - 1) % NP)
    to_next = remote(edge_out.at[1], edge_in.at[0], hsend.at[1], hrecv.at[0], geom, (me + 1) % NP)
    to_prev.start()
    to_next.start()
    pad_ref[HB : HB + C, :] = nodes
    to_prev.wait_recv()
    to_next.wait_recv()
    pad_ref[0:HB, :] = edge_in[0]
    pad_ref[HB + C :, :] = edge_in[1]
    for copy in copies:
        copy.wait_send()
    to_prev.wait_send()
    to_next.wait_send()


def deliver(h, tgt):
    vm = pl.BlockSpec(memory_space=pltpu.VMEM)
    return pl.pallas_call(
        deliver_kernel,
        out_shape=(
            jax.ShapeDtypeStruct((PADDED, D), BF),
            jax.ShapeDtypeStruct((NP, 128), F32),
            jax.ShapeDtypeStruct((1, C), jnp.int32),
        ),
        in_specs=[vm, vm],
        out_specs=(vm, vm, vm),
        scratch_shapes=[
            pltpu.VMEM((NP, CAP, D), BF),
            pltpu.VMEM((NP, CAP, D), BF),
            pltpu.VMEM((NP, 8, 128), F32),
            pltpu.VMEM((NP, 8, 128), F32),
            pltpu.VMEM((2, HB, D), BF),
            pltpu.VMEM((2, HB, D), BF),
            pltpu.VMEM((SLOTS, C), BF),
        ]
        + [pltpu.SemaphoreType.DMA((NP,))] * 4
        + [pltpu.SemaphoreType.DMA((2,))] * 2,
        compiler_params=pltpu.CompilerParams(collective_id=0, has_side_effects=True),
        name="deliver",
    )(h, tgt)


def layer_kernel(
    pad_ref, src_ref, edges_ref, cotn_ref, cote_ref, wei_ref, weo_ref, wni_ref, wno_ref,
    edge_new_ref, node_new_ref, grad_edge_ref, ng_ref, halo_ref,
    hid, post_grad, pre_grad, summed_ref, node_hid_ref, node_pre_ref, node_post_ref, recv_ref, send_ref,
    sel, sel_t, comb, big, slope, normed, inv, ups, total,
):
    step = pl.program_id(0)
    me = lax.axis_index("dom")
    w_self, w_send, w_recv = wei_ref.at[0:D], wei_ref.at[D : 2 * D], wei_ref.at[2 * D : 3 * D]
    w_nself, w_nagg = wni_ref.at[0:D], wni_ref.at[D : 2 * D]
    rows = pl.ds(pl.multiple_of(step * TC, TC), TC)

    @pl.when(step == 0)
    def _():
        comb[0:PADDED, :] = nn(pad_ref[...], w_send[...]).astype(BF)
        sel[:, PADDED:] = (iota((TE, TC), 0) // K == iota((TE, TC), 1)).astype(BF)
        sel_t[PADDED:, :] = (iota((TC, TE), 1) // K == iota((TC, TE), 0)).astype(BF)
        total[...] = jnp.zeros_like(total)

    nodes = pad_ref[pl.ds(pl.multiple_of(HB + step * TC, HB), TC), :]
    edges = edges_ref[...]
    src = src_ref[...] - (me * C - HB)
    sel_t[0:PADDED, :] = (iota((PADDED, TE), 0) == src).astype(BF)
    src_col = jnp.broadcast_to(src.astype(F32), (128, TE)).T.astype(jnp.int32)
    for b in range(PADDED // 128):
        sel[:, b * 128 : (b + 1) * 128] = (src_col == iota((TE, 128), 1) + b * 128).astype(BF)
    comb[PADDED:, :] = nn(nodes, w_recv[...]).astype(BF)

    big[...] = nn(edges, w_self[...]) + nn(sel[...], comb[...])
    for r in range(0, TE, RC):
        v = big[r : r + RC, :]
        s = sigmoid(v)
        h = v * s
        hid[r : r + RC, :] = h.astype(BF)
        slope[r : r + RC, :] = s + h * (1.0 - s)
    big[...] = nn(hid[...], weo_ref[...])
    for r in range(0, TE, RC):
        v = big[r : r + RC, :]
        center = v - jnp.mean(v, axis=-1, keepdims=True)
        i = lax.rsqrt(jnp.mean(center * center, axis=-1, keepdims=True) + 1e-05)
        n = center * i
        normed[r : r + RC, :] = n
        inv[r : r + RC, :] = jnp.broadcast_to(i, (RC, 128))
        edge_new_ref[r : r + RC, :] = (edges_ref[r : r + RC, :].astype(F32) + n).astype(BF)

    four = sel_t[PADDED:, :]
    summed = nn(four, edge_new_ref[...]).astype(BF)
    summed_ref[...] = summed
    v = nn(nodes, w_nself[...]) + nn(summed, w_nagg[...])
    s = sigmoid(v)
    h = v * s
    node_slope = s + h * (1.0 - s)
    node_hid = h.astype(BF)
    node_hid_ref[...] = node_hid
    v = nn(node_hid, wno_ref[...])
    center = v - jnp.mean(v, axis=-1, keepdims=True)
    i = lax.rsqrt(jnp.mean(center * center, axis=-1, keepdims=True) + 1e-05)
    n = center * i
    node_new_ref[...] = (nodes.astype(F32) + n).astype(BF)
    u = cotn_ref[...].astype(F32)
    m1 = jnp.mean(u, axis=-1, keepdims=True)
    m2 = jnp.mean(u * n, axis=-1, keepdims=True)
    node_post_grad = (i * (u - m1 - n * m2)).astype(BF)
    node_post_ref[...] = node_post_grad
    node_pre_grad = (nt(node_post_grad, wno_ref[...]) * node_slope).astype(BF)
    node_pre_ref[...] = node_pre_grad
    spread_grad = nt(node_pre_grad, w_nagg[...]).astype(BF)

    ups[...] = nn(sel[:, PADDED:], spread_grad)
    for r in range(0, TE, RC):
        u = cote_ref[r : r + RC, :].astype(F32) + ups[r : r + RC, :]
        ups[r : r + RC, :] = u
        n = normed[r : r + RC, :]
        m1 = jnp.mean(u, axis=-1, keepdims=True)
        m2 = jnp.mean(u * n, axis=-1, keepdims=True)
        post_grad[r : r + RC, :] = (inv[r : r + RC, 0:1] * (u - m1 - n * m2)).astype(BF)
    big[...] = nt(post_grad[...], weo_ref[...])
    for r in range(0, TE, RC):
        pre_grad[r : r + RC, :] = (big[r : r + RC, :] * slope[r : r + RC, :]).astype(BF)
    g = pre_grad[...]
    big[...] = nt(g, w_self[...])
    for r in range(0, TE, RC):
        grad_edge_ref[r : r + RC, :] = (ups[r : r + RC, :] + big[r : r + RC, :]).astype(BF)
    total[...] += nn(sel_t[0:PADDED, :], g)
    recv_grad = nn(four, g).astype(BF)
    recv_ref[...] = recv_grad
    ng_ref[rows, :] = (
        cotn_ref[...].astype(F32) + nt(node_pre_grad, w_nself[...]) + nt(recv_grad, w_recv[...])
    )

    @pl.when(step == TILES - 1)
    def _():
        t = total[...].astype(BF)
        send_ref[...] = t
        back = nt(t, w_send[...])
        ng_ref[...] += back[HB : HB + C]
        halo_ref[0] = back[0:HB].astype(BF)
        halo_ref[1] = back[HB + C :].astype(BF)


def layer(padded, source, edges, cot_nodes, cot_edges, wei, weo, wni, wno):
    def whole(shape):
        return pl.BlockSpec(shape, lambda i: (0,) * len(shape), pipeline_mode=pl.Buffered(1))

    def tile(rows):
        return pl.BlockSpec((rows, D), lambda i: (i, 0))

    by_edge = jax.ShapeDtypeStruct((C * K, D), BF)
    by_cell = jax.ShapeDtypeStruct((C, D), BF)
    return pl.pallas_call(
        layer_kernel,
        grid=(TILES,),
        out_shape=(
            by_edge, by_cell, by_edge,
            jax.ShapeDtypeStruct((C, D), F32),
            jax.ShapeDtypeStruct((2, HB, D), BF),
            by_edge, by_edge, by_edge, by_cell, by_cell, by_cell, by_cell, by_cell,
            jax.ShapeDtypeStruct((PADDED, D), BF),
        ),
        in_specs=[
            whole((PADDED, D)),
            pl.BlockSpec((1, TE), lambda i: (0, i)),
            tile(TE), tile(TC), tile(TE),
            whole((3 * D, D)), whole((D, D)), whole((2 * D, D)), whole((D, D)),
        ],
        out_specs=(
            tile(TE), tile(TC), tile(TE),
            whole((C, D)), whole((2, HB, D)),
            tile(TE), tile(TE), tile(TE), tile(TC), tile(TC), tile(TC), tile(TC), tile(TC),
            whole((PADDED, D)),
        ),
        scratch_shapes=[
            pltpu.VMEM((TE, SEL), BF),
            pltpu.VMEM((SEL, TE), BF),
            pltpu.VMEM((SEL, D), BF),
            pltpu.VMEM((TE, D), F32),
            pltpu.VMEM((TE, D), F32),
            pltpu.VMEM((TE, D), F32),
            pltpu.VMEM((TE, 128), F32),
            pltpu.VMEM((TE, D), F32),
            pltpu.VMEM((PADDED, D), F32),
        ],
        compiler_params=pltpu.CompilerParams(vmem_limit_bytes=60 * 1024 * 1024),
        name="layer",
    )(padded, source, edges, cot_nodes, cot_edges, wei, weo, wni, wno)


ROWS = SQUARES * D
QW = 128
CW = 2 * QW
ORDER = (4, 5, 6, 2, 1, 3, 0)


def collect_kernel(
    ng_ref, halo_ref, ids_ref,
    edges_hbm, pad_hbm, hid_hbm, post_hbm, pre_hbm, summed_hbm, nhid_hbm, npre_hbm, npost_hbm, recv_hbm, send_hbm,
    back_ref, fin_ref,
    edges, pad, hid, post, pre, summed, nhid, npre, npost, recv_g, send_g,
    hbuf, sback, rback, wown, wsend, pbuf, wsum, r1, p1, r2, r3, fin,
    lsem, hsend, hrecv, bsend, brecv, psend, precv, s1, v1, s2, v2, s3, v3, s4, v4,
):
    geom = lax.axis_index("geom")
    me = lax.axis_index("dom")
    core = geom % 2
    x = geom // 2
    y = me // 4
    z = me % 4
    partner = x * 2 + (1 - core)
    i_me = y * (1 - core) + z * core
    j_me = z * (1 - core) + y * core

    def dom_of(i, j):
        return (i * 4 + j) * (1 - core) + (j * 4 + i) * core

    barrier = pltpu.get_barrier_semaphore()
    signals = NP - 1
    for p in range(1, NP):
        signal(barrier, geom, (me + p) % NP)
    signal(barrier, partner, me)
    for d in range(1, 4):
        signal(barrier, ((x + d) % 4) * 2 + core, me)
    signals += 4

    pairs = (
        (npre_hbm, npre), (pad_hbm, pad), (summed_hbm, summed), (npost_hbm, npost), (nhid_hbm, nhid),
        (recv_hbm, recv_g), (send_hbm, send_g), (post_hbm, post), (hid_hbm, hid), (pre_hbm, pre), (edges_hbm, edges),
    )
    loads = {}
    for n, (far, near) in enumerate(pairs):
        loads[id(near)] = pltpu.make_async_copy(far, near, lsem.at[n])
        loads[id(near)].start()

    def ready(*refs):
        for ref in refs:
            if id(ref) in loads:
                loads.pop(id(ref)).wait()

    scale = 1.0 / math.sqrt(8 * NP * C * K)
    inner = slice(HB, HB + C)
    operands = {
        0: (edges, None, pre), 1: (pad, None, send_g), 2: (pad, inner, recv_g), 3: (hid, None, post),
        4: (pad, inner, npre), 5: (summed, None, npre), 6: (nhid, None, npost),
    }
    pair = {}

    def square(c, q):
        left, cut, right = operands[q]
        ready(left, right)
        rows = left[...] if cut is None else left[cut, :]
        value = (tn(rows, right[:, c * CW : (c + 1) * CW]) * scale).astype(BF)
        low, high = value[:, 0:QW], value[:, QW:CW]
        wown[c, q] = jnp.where(core == 0, low, high)
        wsend[c, q] = jnp.where(core == 0, high, low)
        n = c * SQUARES + q
        pair[c, q] = remote(wsend.at[c, q], pbuf.at[c, q], psend.at[n], precv.at[n], partner, me)

    for q in ORDER[:3]:
        square(0, q)
    pl.semaphore_wait(barrier, signals)
    to_prev = remote(halo_ref.at[0], hbuf.at[1], hsend.at[0], hrecv.at[1], geom, (me + NP - 1) % NP)
    to_next = remote(halo_ref.at[1], hbuf.at[0], hsend.at[1], hrecv.at[0], geom, (me + 1) % NP)
    to_prev.start()
    to_next.start()
    for q in ORDER[:3]:
        pair[0, q].start()
    for q in ORDER[3:5]:
        square(0, q)
        pair[0, q].start()

    blocks = jnp.concatenate(unpack_blocks(ids_ref[...]), axis=0)
    to_prev.wait_recv()
    to_next.wait_recv()
    first = ng_ref[0:HB, :] + hbuf[0].astype(F32)
    last = ng_ref[C - HB :, :] + hbuf[1].astype(F32)
    cells = jnp.concatenate([first, ng_ref[HB : C - HB, :], last], axis=0).astype(BF)
    packed = nn(blocks, cells).astype(BF)
    sback[...] = packed.reshape(NP, CAP, D)
    rback[0] = packed[0:CAP]
    backs = [
        remote(sback.at[p], rback.at[p], bsend.at[p], brecv.at[p], geom, (me + NP - p) % NP)
        for p in range(1, NP)
    ]
    for copy in backs:
        copy.start()

    for q in ORDER[5:]:
        square(0, q)
        pair[0, q].start()

    ones = {}

    def join(c):
        for q in ORDER:
            pair[c, q].wait_recv()
        for k in range(NP):
            parts = []
            at, end = k * PER_DOM, (k + 1) * PER_DOM
            while at < end:
                q, r = divmod(at, D)
                n = min(end - at, D - r)
                parts.append(wown[c, q, r : r + n].astype(F32) + pbuf[c, q, r : r + n].astype(F32))
                at += n
            value = parts[0] if len(parts) == 1 else jnp.concatenate(parts, axis=0)
            i = (k // 4) * (1 - core) + (k % 4) * core
            j = (k % 4) * (1 - core) + (k // 4) * core
            wsum[c, pl.ds(i * 4 + j, 1)] = value.astype(BF).reshape(1, PER_DOM, QW)
        for d in range(1, 4):
            n = c * 3 + d - 1
            ones[c, d] = remote(
                wsum.at[c, pl.ds(((i_me + d) % 4) * 4, 4)], r1.at[c, d - 1], s1.at[n], v1.at[n],
                geom, dom_of((i_me + d) % 4, j_me),
            )
            ones[c, d].start()

    twos, threes, fours = {}, {}, {}

    def narrow(c):
        for d in range(1, 4):
            ones[c, d].wait_recv()
        for j in range(4):
            own = wsum[c, pl.ds(i_me * 4 + j, 1)].reshape(PER_DOM, QW).astype(F32)
            for d in range(3):
                own += r1[c, d, j].astype(F32)
            p1[c, j] = own.astype(BF)
        for d in range(1, 4):
            n = c * 3 + d - 1
            j = (j_me + d) % 4
            twos[c, d] = remote(p1.at[c, j], r2.at[c, d - 1], s2.at[n], v2.at[n], geom, dom_of(i_me, j))
            twos[c, d].start()

    def across(c):
        for d in range(1, 4):
            twos[c, d].wait_recv()
        own = p1[c, pl.ds(j_me, 1)].reshape(PER_DOM, QW).astype(F32)
        for d in range(3):
            own += r2[c, d].astype(F32)
        r3[c, pl.ds(x, 1)] = own.astype(BF).reshape(1, PER_DOM, QW)
        for d in range(1, 4):
            n = c * 3 + d - 1
            threes[c, d] = remote(
                r3.at[c, x], r3.at[c, x], s3.at[n], v3.at[n], ((x + d) % 4) * 2 + core, me
            )
            threes[c, d].start()

    def last_sum(c):
        for d in range(1, 4):
            n = c * 3 + d - 1
            origin = (x + 4 - d) % 4
            remote(r3.at[c, x], r3.at[c, origin], s3.at[n], v3.at[n], origin * 2 + core, me).wait_recv()
        done = r3[c, 0].astype(F32) + r3[c, 1].astype(F32) + r3[c, 2].astype(F32) + r3[c, 3].astype(F32)
        fin[c, pl.ds(core, 1)] = done.astype(BF).reshape(1, PER_DOM, QW)
        fours[c] = remote(fin.at[c, core], fin.at[c, core], s4.at[c], v4.at[c], partner, me)
        fours[c].start()

    join(0)
    for q in ORDER:
        square(1, q)
        pair[1, q].start()
    join(1)
    narrow(0)
    narrow(1)
    across(0)
    across(1)
    for copy in backs:
        copy.wait_recv()
    last_sum(0)
    last_sum(1)
    for c in range(2):
        remote(fin.at[c, core], fin.at[c, 1 - core], s4.at[c], v4.at[c], partner, me).wait_recv()
    back_ref[...] = rback[...].reshape(SLOTS, D)
    for c in range(2):
        for q in range(2):
            fin_ref[:, c * CW + q * QW : c * CW + (q + 1) * QW] = fin[c, q]
    groups = (pair, ones, twos, threes, fours)
    for copy in [to_prev, to_next] + backs + [copy for group in groups for copy in group.values()]:
        copy.wait_send()


def finish_kernel(back_ref, slot_ref, fin_ref, grad_ref, out_ref):
    grad_ref[...] = tn(pack_matrix(slot_ref[...]), back_ref[...]).astype(BF)
    out_ref[...] = fin_ref[...].astype(F32)


def finish(back, slot, fin):
    vm = pl.BlockSpec(memory_space=pltpu.VMEM)
    return pl.pallas_call(
        finish_kernel,
        out_shape=(jax.ShapeDtypeStruct((C, D), BF), jax.ShapeDtypeStruct((PER_DOM, D), F32)),
        in_specs=[vm] * 3,
        out_specs=(vm, vm),
        name="finish",
    )(back, slot, fin)


def collect(ng, halo, ids, *operands):
    vm = pl.BlockSpec(memory_space=pltpu.VMEM)
    hbm = pl.BlockSpec(memory_space=pl.ANY)
    dma = pltpu.SemaphoreType.DMA
    return pl.pallas_call(
        collect_kernel,
        out_shape=(
            jax.ShapeDtypeStruct((SLOTS, D), BF),
            jax.ShapeDtypeStruct((PER_DOM, D), BF),
        ),
        in_specs=[vm] * 3 + [hbm] * len(operands),
        out_specs=(vm, vm),
        scratch_shapes=[pltpu.VMEM(a.shape, a.dtype) for a in operands]
        + [
            pltpu.VMEM((2, HB, D), BF),
            pltpu.VMEM((NP, CAP, D), BF),
            pltpu.VMEM((NP, CAP, D), BF),
            pltpu.VMEM((2, SQUARES, D, QW), BF),
            pltpu.VMEM((2, SQUARES, D, QW), BF),
            pltpu.VMEM((2, SQUARES, D, QW), BF),
            pltpu.VMEM((2, NP, PER_DOM, QW), BF),
            pltpu.VMEM((2, 3, 4, PER_DOM, QW), BF),
            pltpu.VMEM((2, 4, PER_DOM, QW), BF),
            pltpu.VMEM((2, 3, PER_DOM, QW), BF),
            pltpu.VMEM((2, 4, PER_DOM, QW), BF),
            pltpu.VMEM((2, 2, PER_DOM, QW), BF),
            dma((len(operands),)), dma((2,)), dma((2,)), dma((NP,)), dma((NP,)),
            dma((2 * SQUARES,)), dma((2 * SQUARES,)), dma((6,)), dma((6,)),
            dma((6,)), dma((6,)), dma((6,)), dma((6,)), dma((2,)), dma((2,)),
        ],
        compiler_params=pltpu.CompilerParams(
            collective_id=1, has_side_effects=True, vmem_limit_bytes=60 * 1024 * 1024
        ),
        name="collect",
    )(ng, halo, ids, *operands)


def local(
    h_in, edge_in, new_index, source, w_edge_in, w_edge_out, w_node_in, w_node_out, cot_nodes, cot_edges
):
    padded, ids, slot = deliver(h_in[0], new_index)
    edge_new, node_new, grad_edge, ng, halo, hid, post, pre, summed, nhid, npre, npost, recv, send = layer(
        padded, source, edge_in[0], cot_nodes[0], cot_edges[0], w_edge_in, w_edge_out, w_node_in, w_node_out
    )
    back, fin = collect(
        ng, halo, ids, edge_in[0], padded, hid, post, pre, summed, nhid, npre, npost, recv, send
    )
    grad_in, weight_grads = finish(back, slot, fin)
    return (node_new[None], edge_new[None], grad_in[None], grad_edge[None], weight_grads)


def solution(mesh):
    return jax.shard_map(
        local,
        mesh=mesh,
        in_specs=(
            P("geom", "dom", None),
            P("geom", "dom", None),
            P("geom", "dom"),
            P("geom", "dom"),
            P(),
            P(),
            P(),
            P(),
            P("geom", "dom", None),
            P("geom", "dom", None),
        ),
        out_specs=(
            P("geom", "dom", None),
            P("geom", "dom", None),
            P("geom", "dom", None),
            P("geom", "dom", None),
            P("dom", None),
        ),
        check_vma=False,
    )
```

```python
import functools
import math

import jax
import jax.numpy as jnp
from jax import lax
from jax.experimental import pallas as pl
from jax.experimental.pallas import tpu as pltpu
from jax.sharding import PartitionSpec as P

MESH = pl.DeviceIdType.MESH
BF = jnp.bfloat16
F32 = jnp.float32

D = 512
K = 4
C = 512
HB = 64
PADDED = C + 2 * HB
NP = 16
CAP = 48
SLOTS = NP * CAP
TC = 128
TE = TC * K
TILES = C // TC
SEL = PADDED + TC
RC = 64
SQUARES = 7
PER_DOM = SQUARES * D // NP


def nn(a, b):
    return jnp.dot(a, b, preferred_element_type=F32)


def nt(a, b):
    return lax.dot_general(a, b, (((1,), (1,)), ((), ())), preferred_element_type=F32)


def tn(a, b):
    return lax.dot_general(a, b, (((0,), (0,)), ((), ())), preferred_element_type=F32)


def sigmoid(v):
    return 0.5 * jnp.tanh(0.5 * v) + 0.5


def iota(shape, dim):
    return lax.broadcasted_iota(jnp.int32, shape, dim)


def remote(src, dst, send, recv, geom, dom):
    return pltpu.make_async_remote_copy(
        src_ref=src,
        dst_ref=dst,
        send_sem=send,
        recv_sem=recv,
        device_id=(geom, dom),
        device_id_type=MESH,
    )


def signal(sem, geom, dom):
    pl.semaphore_signal(sem, inc=1, device_id=(geom, dom), device_id_type=MESH)


def pack_matrix(slot):
    return (iota((SLOTS, C), 0) == slot).astype(BF)


def unpack_blocks(ids):
    turned = ids.T
    lanes = iota((CAP, C), 1).astype(F32)
    return [(turned[0:CAP, p : p + 1] == lanes).astype(BF) for p in range(NP)]


def deliver_kernel(
    h_ref, tgt_ref, pad_ref, ids_ref, slot_ref,
    sbuf, rbuf, sids, rids, edge_out, edge_in, mt,
    send, recv, isend, irecv, hsend, hrecv,
):
    geom = lax.axis_index("geom")
    me = lax.axis_index("dom")
    barrier = pltpu.get_barrier_semaphore()
    for p in range(1, NP):
        signal(barrier, geom, (me + p) % NP)

    tgt = tgt_ref[...]
    off = ((tgt >> 9) - me) & (NP - 1)
    row = tgt & (C - 1)
    owned = (iota((NP, C), 0) == off).astype(F32)
    upper = (iota((C, C), 0) < iota((C, C), 1)).astype(BF)
    before = nn(owned.astype(BF), upper)
    rank = jnp.sum(owned * before, axis=0, keepdims=True).astype(jnp.int32)
    slot = off * CAP + rank
    slot_ref[...] = slot
    ranked = (iota((128, C), 0) == rank).astype(BF)
    high = (row >> 5).astype(F32)
    low = (row & 31).astype(F32)
    coded = nt(jnp.concatenate([owned * high, owned * low, owned], axis=0).astype(BF), ranked)
    ids = 32.0 * coded[0:NP] + coded[NP : 2 * NP] + coded[2 * NP :] - 1.0
    for p in range(NP):
        sids[p] = jnp.broadcast_to(ids[p : p + 1, :], (8, 128))
    packed = nn(pack_matrix(slot), h_ref[...]).astype(BF)
    sbuf[...] = packed.reshape(NP, CAP, D)
    rbuf[0] = packed[0:CAP]

    pl.semaphore_wait(barrier, NP - 1)
    copies = []
    for p in range(1, NP):
        peer = (me + p) % NP
        copies.append(remote(sids.at[p], rids.at[p], isend.at[p], irecv.at[p], geom, peer))
        copies.append(remote(sbuf.at[p], rbuf.at[p], send.at[p], recv.at[p], geom, peer))
    for copy in copies:
        copy.start()
    for copy in copies[0::2]:
        copy.wait_recv()
    got = jnp.concatenate([ids[0:1]] + [rids[p, 0:1, :] for p in range(1, NP)], axis=0)
    ids_ref[...] = got
    for p, block in enumerate(unpack_blocks(got)):
        mt[pl.ds(p * CAP, CAP), :] = block
    for copy in copies[1::2]:
        copy.wait_recv()
    nodes = tn(mt[...], rbuf[...].reshape(SLOTS, D)).astype(BF)
    edge_out[0] = nodes[0:HB]
    edge_out[1] = nodes[C - HB : C]
    to_prev = remote(edge_out.at[0], edge_in.at[1], hsend.at[0], hrecv.at[1], geom, (me + NP - 1) % NP)
    to_next = remote(edge_out.at[1], edge_in.at[0], hsend.at[1], hrecv.at[0], geom, (me + 1) % NP)
    to_prev.start()
    to_next.start()
    pad_ref[HB : HB + C, :] = nodes
    to_prev.wait_recv()
    to_next.wait_recv()
    pad_ref[0:HB, :] = edge_in[0]
    pad_ref[HB + C :, :] = edge_in[1]
    for copy in copies:
        copy.wait_send()
    to_prev.wait_send()
    to_next.wait_send()


def deliver(h, tgt):
    vm = pl.BlockSpec(memory_space=pltpu.VMEM)
    return pl.pallas_call(
        deliver_kernel,
        out_shape=(
            jax.ShapeDtypeStruct((PADDED, D), BF),
            jax.ShapeDtypeStruct((NP, 128), F32),
            jax.ShapeDtypeStruct((1, C), jnp.int32),
        ),
        in_specs=[vm, vm],
        out_specs=(vm, vm, vm),
        scratch_shapes=[
            pltpu.VMEM((NP, CAP, D), BF),
            pltpu.VMEM((NP, CAP, D), BF),
            pltpu.VMEM((NP, 8, 128), F32),
            pltpu.VMEM((NP, 8, 128), F32),
            pltpu.VMEM((2, HB, D), BF),
            pltpu.VMEM((2, HB, D), BF),
            pltpu.VMEM((SLOTS, C), BF),
        ]
        + [pltpu.SemaphoreType.DMA((NP,))] * 4
        + [pltpu.SemaphoreType.DMA((2,))] * 2,
        compiler_params=pltpu.CompilerParams(collective_id=0, has_side_effects=True),
        name="deliver",
    )(h, tgt)


def layer_kernel(
    pad_ref, src_ref, edges_ref, cotn_ref, cote_ref, wei_ref, weo_ref, wni_ref, wno_ref,
    edge_new_ref, node_new_ref, grad_edge_ref, ng_ref, halo_ref,
    hid, post_grad, pre_grad, summed_ref, node_hid_ref, node_pre_ref, node_post_ref, recv_ref, send_ref,
    sel, sel_t, comb, big, slope, normed, inv, ups, total,
):
    step = pl.program_id(0)
    me = lax.axis_index("dom")
    w_self, w_send, w_recv = wei_ref.at[0:D], wei_ref.at[D : 2 * D], wei_ref.at[2 * D : 3 * D]
    w_nself, w_nagg = wni_ref.at[0:D], wni_ref.at[D : 2 * D]
    rows = pl.ds(pl.multiple_of(step * TC, TC), TC)

    @pl.when(step == 0)
    def _():
        comb[0:PADDED, :] = nn(pad_ref[...], w_send[...]).astype(BF)
        sel[:, PADDED:] = (iota((TE, TC), 0) // K == iota((TE, TC), 1)).astype(BF)
        sel_t[PADDED:, :] = (iota((TC, TE), 1) // K == iota((TC, TE), 0)).astype(BF)
        total[...] = jnp.zeros_like(total)

    nodes = pad_ref[pl.ds(pl.multiple_of(HB + step * TC, HB), TC), :]
    edges = edges_ref[...]
    src = src_ref[...] - (me * C - HB)
    sel_t[0:PADDED, :] = (iota((PADDED, TE), 0) == src).astype(BF)
    src_col = jnp.broadcast_to(src.astype(F32), (128, TE)).T.astype(jnp.int32)
    for b in range(PADDED // 128):
        sel[:, b * 128 : (b + 1) * 128] = (src_col == iota((TE, 128), 1) + b * 128).astype(BF)
    comb[PADDED:, :] = nn(nodes, w_recv[...]).astype(BF)

    big[...] = nn(edges, w_self[...]) + nn(sel[...], comb[...])
    for r in range(0, TE, RC):
        v = big[r : r + RC, :]
        s = sigmoid(v)
        h = v * s
        hid[r : r + RC, :] = h.astype(BF)
        slope[r : r + RC, :] = s + h * (1.0 - s)
    big[...] = nn(hid[...], weo_ref[...])
    for r in range(0, TE, RC):
        v = big[r : r + RC, :]
        center = v - jnp.mean(v, axis=-1, keepdims=True)
        i = lax.rsqrt(jnp.mean(center * center, axis=-1, keepdims=True) + 1e-05)
        n = center * i
        normed[r : r + RC, :] = n
        inv[r : r + RC, :] = jnp.broadcast_to(i, (RC, 128))
        edge_new_ref[r : r + RC, :] = (edges_ref[r : r + RC, :].astype(F32) + n).astype(BF)

    four = sel_t[PADDED:, :]
    summed = nn(four, edge_new_ref[...]).astype(BF)
    summed_ref[...] = summed
    v = nn(nodes, w_nself[...]) + nn(summed, w_nagg[...])
    s = sigmoid(v)
    h = v * s
    node_slope = s + h * (1.0 - s)
    node_hid = h.astype(BF)
    node_hid_ref[...] = node_hid
    v = nn(node_hid, wno_ref[...])
    center = v - jnp.mean(v, axis=-1, keepdims=True)
    i = lax.rsqrt(jnp.mean(center * center, axis=-1, keepdims=True) + 1e-05)
    n = center * i
    node_new_ref[...] = (nodes.astype(F32) + n).astype(BF)
    u = cotn_ref[...].astype(F32)
    m1 = jnp.mean(u, axis=-1, keepdims=True)
    m2 = jnp.mean(u * n, axis=-1, keepdims=True)
    node_post_grad = (i * (u - m1 - n * m2)).astype(BF)
    node_post_ref[...] = node_post_grad
    node_pre_grad = (nt(node_post_grad, wno_ref[...]) * node_slope).astype(BF)
    node_pre_ref[...] = node_pre_grad
    spread_grad = nt(node_pre_grad, w_nagg[...]).astype(BF)

    ups[...] = nn(sel[:, PADDED:], spread_grad)
    for r in range(0, TE, RC):
        u = cote_ref[r : r + RC, :].astype(F32) + ups[r : r + RC, :]
        ups[r : r + RC, :] = u
        n = normed[r : r + RC, :]
        m1 = jnp.mean(u, axis=-1, keepdims=True)
        m2 = jnp.mean(u * n, axis=-1, keepdims=True)
        post_grad[r : r + RC, :] = (inv[r : r + RC, 0:1] * (u - m1 - n * m2)).astype(BF)
    big[...] = nt(post_grad[...], weo_ref[...])
    for r in range(0, TE, RC):
        pre_grad[r : r + RC, :] = (big[r : r + RC, :] * slope[r : r + RC, :]).astype(BF)
    g = pre_grad[...]
    big[...] = nt(g, w_self[...])
    for r in range(0, TE, RC):
        grad_edge_ref[r : r + RC, :] = (ups[r : r + RC, :] + big[r : r + RC, :]).astype(BF)
    total[...] += nn(sel_t[0:PADDED, :], g)
    recv_grad = nn(four, g).astype(BF)
    recv_ref[...] = recv_grad
    ng_ref[rows, :] = (
        cotn_ref[...].astype(F32) + nt(node_pre_grad, w_nself[...]) + nt(recv_grad, w_recv[...])
    )

    @pl.when(step == TILES - 1)
    def _():
        t = total[...].astype(BF)
        send_ref[...] = t
        back = nt(t, w_send[...])
        ng_ref[...] += back[HB : HB + C]
        halo_ref[0] = back[0:HB].astype(BF)
        halo_ref[1] = back[HB + C :].astype(BF)


def layer(padded, source, edges, cot_nodes, cot_edges, wei, weo, wni, wno):
    def whole(shape):
        return pl.BlockSpec(shape, lambda i: (0,) * len(shape), pipeline_mode=pl.Buffered(1))

    def tile(rows):
        return pl.BlockSpec((rows, D), lambda i: (i, 0))

    by_edge = jax.ShapeDtypeStruct((C * K, D), BF)
    by_cell = jax.ShapeDtypeStruct((C, D), BF)
    return pl.pallas_call(
        layer_kernel,
        grid=(TILES,),
        out_shape=(
            by_edge, by_cell, by_edge,
            jax.ShapeDtypeStruct((C, D), F32),
            jax.ShapeDtypeStruct((2, HB, D), BF),
            by_edge, by_edge, by_edge, by_cell, by_cell, by_cell, by_cell, by_cell,
            jax.ShapeDtypeStruct((PADDED, D), BF),
        ),
        in_specs=[
            whole((PADDED, D)),
            pl.BlockSpec((1, TE), lambda i: (0, i)),
            tile(TE), tile(TC), tile(TE),
            whole((3 * D, D)), whole((D, D)), whole((2 * D, D)), whole((D, D)),
        ],
        out_specs=(
            tile(TE), tile(TC), tile(TE),
            whole((C, D)), whole((2, HB, D)),
            tile(TE), tile(TE), tile(TE), tile(TC), tile(TC), tile(TC), tile(TC), tile(TC),
            whole((PADDED, D)),
        ),
        scratch_shapes=[
            pltpu.VMEM((TE, SEL), BF),
            pltpu.VMEM((SEL, TE), BF),
            pltpu.VMEM((SEL, D), BF),
            pltpu.VMEM((TE, D), F32),
            pltpu.VMEM((TE, D), F32),
            pltpu.VMEM((TE, D), F32),
            pltpu.VMEM((TE, 128), F32),
            pltpu.VMEM((TE, D), F32),
            pltpu.VMEM((PADDED, D), F32),
        ],
        compiler_params=pltpu.CompilerParams(vmem_limit_bytes=60 * 1024 * 1024),
        name="layer",
    )(padded, source, edges, cot_nodes, cot_edges, wei, weo, wni, wno)


ROWS = SQUARES * D
QW = 128
CW = 2 * QW
EARLY = 10
PART = 64
STARTS = (0, 64, 128, 160)


def collect_kernel(
    ng_ref, halo_ref, ids_ref,
    edges_hbm, pad_hbm, hid_hbm, post_hbm, pre_hbm, summed_hbm, nhid_hbm, npre_hbm, npost_hbm, recv_hbm, send_hbm,
    back_ref, fin_ref,
    edges, pad, hid, post, pre, summed, nhid, npre, npost, recv_g, send_g,
    hbuf, sback, rback, wown, wsend, pbuf, wsum, r1, p1, r2, r3, fin, wx, rx, px, ri, ag,
    lsem, hsend, hrecv, bsend, brecv, psend, precv, s1, v1, s2, v2, s3, v3, s4, v4, sx, vx, si, vi, sg, vg,
):
    geom = lax.axis_index("geom")
    me = lax.axis_index("dom")
    core = geom % 2
    x = geom // 2
    y = me // 4
    z = me % 4
    partner = x * 2 + (1 - core)
    i_me = y * (1 - core) + z * core
    j_me = z * (1 - core) + y * core

    def dom_of(i, j):
        return (i * 4 + j) * (1 - core) + (j * 4 + i) * core

    barrier = pltpu.get_barrier_semaphore()
    signals = NP - 1
    for p in range(1, NP):
        signal(barrier, geom, (me + p) % NP)
    for d in range(1, 8):
        signal(barrier, (geom + d) % 8, me)
        signals += 1

    pairs = (
        (npre_hbm, npre), (pad_hbm, pad), (summed_hbm, summed), (npost_hbm, npost), (nhid_hbm, nhid),
        (post_hbm, post), (hid_hbm, hid), (recv_hbm, recv_g), (send_hbm, send_g), (pre_hbm, pre), (edges_hbm, edges),
    )
    loads = {}
    for n, (far, near) in enumerate(pairs):
        loads[id(near)] = pltpu.make_async_copy(far, near, lsem.at[n])
        loads[id(near)].start()

    def ready(*refs):
        for ref in refs:
            if id(ref) in loads:
                loads.pop(id(ref)).wait()

    scale = 1.0 / math.sqrt(8 * NP * C * K)
    inner = slice(HB, HB + C)
    operands = {
        0: (edges, None, pre), 1: (pad, None, send_g), 2: (pad, inner, recv_g), 3: (hid, None, post),
        4: (pad, inner, npre), 5: (summed, None, npre), 6: (nhid, None, npost),
    }
    pair = {}

    def square(q):
        left, cut, right = operands[q]
        ready(left, right)
        rows = left[...] if cut is None else left[cut, :]
        value = (tn(rows, right[...]) * scale).astype(BF)
        for c in range(2):
            low, high = value[:, c * CW : c * CW + QW], value[:, c * CW + QW : (c + 1) * CW]
            wown[c, q] = jnp.where(core == 0, low, high)
            wsend[c, q] = jnp.where(core == 0, high, low)
            n = c * SQUARES + q
            pair[c, q] = remote(wsend.at[c, q], pbuf.at[c, q], psend.at[n], precv.at[n], partner, me)

    def reduced_block(c, k):
        parts = []
        at, end = k * PER_DOM, (k + 1) * PER_DOM
        while at < end:
            q, r = divmod(at, D)
            n = min(end - at, D - r)
            parts.append(wown[c, q, r : r + n].astype(F32) + pbuf[c, q, r : r + n].astype(F32))
            at += n
        value = parts[0] if len(parts) == 1 else jnp.concatenate(parts, axis=0)
        return value.astype(BF)

    seen = set()

    def joined(c, squares):
        for q in squares:
            if (c, q) not in seen:
                seen.add((c, q))
                pair[c, q].wait_recv()

    ones, xs, ys = {}, [], []

    def join(c):
        joined(c, range(SQUARES))
        for k in range(NP):
            i = (k // 4) * (1 - core) + (k % 4) * core
            j = (k % 4) * (1 - core) + (k // 4) * core
            wsum[pl.ds(i * 4 + j, 1)] = reduced_block(c, k).reshape(1, PER_DOM, QW)
        for d in range(1, 4):
            to = (i_me + d) % 4
            ones[d] = remote(
                wsum.at[pl.ds(to * 4, 4)], r1.at[d - 1], s1.at[d - 1], v1.at[d - 1], geom, dom_of(to, j_me)
            )
            ones[d].start()

    def join_x(c, low, high, squares):
        joined(c, squares)
        for k in range(low, high):
            value = reduced_block(c, k)
            for n, r in enumerate(STARTS):
                wx[n, k] = value[r : r + PART]
        for d in range(1, 4):
            to = (x + d) % 4
            n = len(xs)
            xs.append(
                remote(
                    wx.at[to, low:high], rx.at[d - 1, low:high], sx.at[n], vx.at[n], to * 2 + core, me
                )
            )
            xs[-1].start()

    def narrow_x():
        for copy in xs:
            copy.wait_recv()
        own = wx[pl.ds(x, 1)].reshape(NP, PART, QW).astype(F32)
        for d in range(3):
            own += rx[d].astype(F32)
        px[...] = own.astype(BF)
        for d in range(1, NP):
            to = (me + d) % NP
            ys.append(remote(px.at[to], ri.at[d - 1], si.at[d - 1], vi.at[d - 1], geom, to))
            ys[-1].start()

    gathers = []

    def narrow_dom():
        for copy in ys:
            copy.wait_recv()
        own = px[pl.ds(me, 1)].reshape(PART, QW).astype(F32)
        for d in range(NP - 1):
            own += ri[d].astype(F32)
        ag[pl.ds(geom, 1)] = own.astype(BF).reshape(1, PART, QW)
        for d in range(1, 8):
            gathers.append(
                remote(ag.at[geom], ag.at[geom], sg.at[d - 1], vg.at[d - 1], (geom + d) % 8, me)
            )
            gathers[-1].start()

    twos, threes = {}, {}

    def narrow():
        for d in range(1, 4):
            ones[d].wait_recv()
        for j in range(4):
            own = wsum[pl.ds(i_me * 4 + j, 1)].reshape(PER_DOM, QW).astype(F32)
            for d in range(3):
                own += r1[d, j].astype(F32)
            p1[j] = own.astype(BF)
        for d in range(1, 4):
            j = (j_me + d) % 4
            twos[d] = remote(p1.at[j], r2.at[d - 1], s2.at[d - 1], v2.at[d - 1], geom, dom_of(i_me, j))
            twos[d].start()

    def across():
        for d in range(1, 4):
            twos[d].wait_recv()
        own = p1[pl.ds(j_me, 1)].reshape(PER_DOM, QW).astype(F32)
        for d in range(3):
            own += r2[d].astype(F32)
        r3[pl.ds(x, 1)] = own.astype(BF).reshape(1, PER_DOM, QW)
        for d in range(1, 4):
            threes[d] = remote(r3.at[x], r3.at[x], s3.at[d - 1], v3.at[d - 1], ((x + d) % 4) * 2 + core, me)
            threes[d].start()

    def send_pairs(*squares):
        for c in (1, 0):
            for q in squares:
                pair[c, q].start()

    for q in (4, 5, 6):
        square(q)
    pl.semaphore_wait(barrier, signals)
    send_pairs(4, 5, 6)
    to_prev = remote(halo_ref.at[0], hbuf.at[1], hsend.at[0], hrecv.at[1], geom, (me + NP - 1) % NP)
    to_next = remote(halo_ref.at[1], hbuf.at[0], hsend.at[1], hrecv.at[0], geom, (me + 1) % NP)
    to_prev.start()
    to_next.start()
    square(3)
    send_pairs(3)
    join_x(1, EARLY, NP, (4, 5, 6))
    for q in (2, 1, 0):
        square(q)
        send_pairs(q)
    join_x(1, 0, EARLY, range(SQUARES))
    join(0)

    blocks = jnp.concatenate(unpack_blocks(ids_ref[...]), axis=0)
    to_prev.wait_recv()
    to_next.wait_recv()
    first = ng_ref[0:HB, :] + hbuf[0].astype(F32)
    last = ng_ref[C - HB :, :] + hbuf[1].astype(F32)
    cells = jnp.concatenate([first, ng_ref[HB : C - HB, :], last], axis=0).astype(BF)
    packed = nn(blocks, cells).astype(BF)
    sback[...] = packed.reshape(NP, CAP, D)
    rback[0] = packed[0:CAP]
    backs = [
        remote(sback.at[p], rback.at[p], bsend.at[p], brecv.at[p], geom, (me + NP - p) % NP)
        for p in range(1, NP)
    ]
    for copy in backs:
        copy.start()

    narrow_x()
    narrow()
    across()
    narrow_dom()
    for copy in backs:
        copy.wait_recv()
    back_ref[...] = rback[...].reshape(SLOTS, D)
    for d in range(1, 4):
        origin = (x + 4 - d) % 4
        remote(r3.at[x], r3.at[origin], s3.at[d - 1], v3.at[d - 1], origin * 2 + core, me).wait_recv()
    done = r3[0].astype(F32) + r3[1].astype(F32) + r3[2].astype(F32) + r3[3].astype(F32)
    fin[pl.ds(core, 1)] = done.astype(BF).reshape(1, PER_DOM, QW)
    four = remote(fin.at[core], fin.at[core], s4, v4, partner, me)
    four.start()
    for d in range(1, 8):
        origin = (geom + 8 - d) % 8
        remote(ag.at[geom], ag.at[origin], sg.at[d - 1], vg.at[d - 1], origin, me).wait_recv()
    for q in range(2):
        for n, r in enumerate(STARTS):
            fin_ref[r : r + PART, CW + q * QW : CW + (q + 1) * QW] = ag[n * 2 + q]
    remote(fin.at[core], fin.at[1 - core], s4, v4, partner, me).wait_recv()
    for q in range(2):
        fin_ref[:, q * QW : (q + 1) * QW] = fin[q]
    groups = (pair, ones, twos, threes)
    for copy in [to_prev, to_next, four] + backs + xs + ys + gathers:
        copy.wait_send()
    for group in groups:
        for copy in group.values():
            copy.wait_send()


def finish_kernel(back_ref, slot_ref, fin_ref, grad_ref, out_ref):
    grad_ref[...] = tn(pack_matrix(slot_ref[...]), back_ref[...]).astype(BF)
    out_ref[...] = fin_ref[...].astype(F32)


def finish(back, slot, fin):
    vm = pl.BlockSpec(memory_space=pltpu.VMEM)
    return pl.pallas_call(
        finish_kernel,
        out_shape=(jax.ShapeDtypeStruct((C, D), BF), jax.ShapeDtypeStruct((PER_DOM, D), F32)),
        in_specs=[vm] * 3,
        out_specs=(vm, vm),
        name="finish",
    )(back, slot, fin)


def collect(ng, halo, ids, *operands):
    vm = pl.BlockSpec(memory_space=pltpu.VMEM)
    hbm = pl.BlockSpec(memory_space=pl.ANY)
    dma = pltpu.SemaphoreType.DMA
    return pl.pallas_call(
        collect_kernel,
        out_shape=(
            jax.ShapeDtypeStruct((SLOTS, D), BF),
            jax.ShapeDtypeStruct((PER_DOM, D), BF),
        ),
        in_specs=[vm] * 3 + [hbm] * len(operands),
        out_specs=(vm, vm),
        scratch_shapes=[pltpu.VMEM(a.shape, a.dtype) for a in operands]
        + [
            pltpu.VMEM((2, HB, D), BF),
            pltpu.VMEM((NP, CAP, D), BF),
            pltpu.VMEM((NP, CAP, D), BF),
            pltpu.VMEM((2, SQUARES, D, QW), BF),
            pltpu.VMEM((2, SQUARES, D, QW), BF),
            pltpu.VMEM((2, SQUARES, D, QW), BF),
            pltpu.VMEM((NP, PER_DOM, QW), BF),
            pltpu.VMEM((3, 4, PER_DOM, QW), BF),
            pltpu.VMEM((4, PER_DOM, QW), BF),
            pltpu.VMEM((3, PER_DOM, QW), BF),
            pltpu.VMEM((4, PER_DOM, QW), BF),
            pltpu.VMEM((2, PER_DOM, QW), BF),
            pltpu.VMEM((4, NP, PART, QW), BF),
            pltpu.VMEM((3, NP, PART, QW), BF),
            pltpu.VMEM((NP, PART, QW), BF),
            pltpu.VMEM((NP - 1, PART, QW), BF),
            pltpu.VMEM((8, PART, QW), BF),
            dma((len(operands),)), dma((2,)), dma((2,)), dma((NP,)), dma((NP,)),
            dma((2 * SQUARES,)), dma((2 * SQUARES,)), dma((3,)), dma((3,)),
            dma((3,)), dma((3,)), dma((3,)), dma((3,)), dma, dma,
            dma((6,)), dma((6,)), dma((NP - 1,)), dma((NP - 1,)), dma((7,)), dma((7,)),
        ],
        compiler_params=pltpu.CompilerParams(
            collective_id=1, has_side_effects=True, vmem_limit_bytes=60 * 1024 * 1024
        ),
        name="collect",
    )(ng, halo, ids, *operands)


def local(
    h_in, edge_in, new_index, source, w_edge_in, w_edge_out, w_node_in, w_node_out, cot_nodes, cot_edges
):
    padded, ids, slot = deliver(h_in[0], new_index)
    edge_new, node_new, grad_edge, ng, halo, hid, post, pre, summed, nhid, npre, npost, recv, send = layer(
        padded, source, edge_in[0], cot_nodes[0], cot_edges[0], w_edge_in, w_edge_out, w_node_in, w_node_out
    )
    back, fin = collect(
        ng, halo, ids, edge_in[0], padded, hid, post, pre, summed, nhid, npre, npost, recv, send
    )
    grad_in, weight_grads = finish(back, slot, fin)
    return (node_new[None], edge_new[None], grad_in[None], grad_edge[None], weight_grads)


def solution(mesh):
    return jax.shard_map(
        local,
        mesh=mesh,
        in_specs=(
            P("geom", "dom", None),
            P("geom", "dom", None),
            P("geom", "dom"),
            P("geom", "dom"),
            P(),
            P(),
            P(),
            P(),
            P("geom", "dom", None),
            P("geom", "dom", None),
        ),
        out_specs=(
            P("geom", "dom", None),
            P("geom", "dom", None),
            P("geom", "dom", None),
            P("geom", "dom", None),
            P("dom", None),
        ),
        check_vma=False,
    )
```

```python
import functools
import math

import jax
import jax.numpy as jnp
from jax import lax
from jax.experimental import pallas as pl
from jax.experimental.pallas import tpu as pltpu
from jax.sharding import PartitionSpec as P

MESH = pl.DeviceIdType.MESH
BF = jnp.bfloat16
F32 = jnp.float32

D = 512
K = 4
C = 512
HB = 64
PADDED = C + 2 * HB
NP = 16
CAP = 48
SLOTS = NP * CAP
TC = 128
TE = TC * K
TILES = C // TC
SEL = PADDED + TC
RC = 64
SQUARES = 7
PER_DOM = SQUARES * D // NP


def nn(a, b):
    return jnp.dot(a, b, preferred_element_type=F32)


def nt(a, b):
    return lax.dot_general(a, b, (((1,), (1,)), ((), ())), preferred_element_type=F32)


def tn(a, b):
    return lax.dot_general(a, b, (((0,), (0,)), ((), ())), preferred_element_type=F32)


def sigmoid(v):
    return 0.5 * jnp.tanh(0.5 * v) + 0.5


def iota(shape, dim):
    return lax.broadcasted_iota(jnp.int32, shape, dim)


def remote(src, dst, send, recv, geom, dom):
    return pltpu.make_async_remote_copy(
        src_ref=src,
        dst_ref=dst,
        send_sem=send,
        recv_sem=recv,
        device_id=(geom, dom),
        device_id_type=MESH,
    )


def signal(sem, geom, dom):
    pl.semaphore_signal(sem, inc=1, device_id=(geom, dom), device_id_type=MESH)


def pack_matrix(slot):
    return (iota((SLOTS, C), 0) == slot).astype(BF)


def unpack_blocks(ids):
    turned = ids.T
    lanes = iota((CAP, C), 1).astype(F32)
    return [(turned[0:CAP, p : p + 1] == lanes).astype(BF) for p in range(NP)]


def deliver_kernel(
    h_hbm, tgt_hbm, src_hbm, edges_hbm, w_hbm,
    pad_ref, ids_ref, slot_ref, sel_ref, self_ref,
    h_ref, tgt_ref, src_ref, edges, w_self, sbuf, rbuf, sids, rids, edge_out, edge_in, mt,
    send, recv, isend, irecv, hsend, hrecv, lsem,
):
    geom = lax.axis_index("geom")
    me = lax.axis_index("dom")
    barrier = pltpu.get_barrier_semaphore()
    for p in range(1, NP):
        signal(barrier, geom, (me + p) % NP)

    loads = [
        pltpu.make_async_copy(far, near, lsem.at[n])
        for n, (far, near) in enumerate(
            ((tgt_hbm, tgt_ref), (h_hbm, h_ref), (edges_hbm, edges), (w_hbm.at[0:D], w_self), (src_hbm, src_ref))
        )
    ]
    for load in loads:
        load.start()
    loads[0].wait()
    tgt = tgt_ref[...]
    off = ((tgt >> 9) - me) & (NP - 1)
    row = tgt & (C - 1)
    owned = (iota((NP, C), 0) == off).astype(F32)
    upper = (iota((C, C), 0) < iota((C, C), 1)).astype(BF)
    before = nn(owned.astype(BF), upper)
    rank = jnp.sum(owned * before, axis=0, keepdims=True).astype(jnp.int32)
    slot = off * CAP + rank
    slot_ref[...] = slot
    ranked = (iota((128, C), 0) == rank).astype(BF)
    high = (row >> 5).astype(F32)
    low = (row & 31).astype(F32)
    coded = nt(jnp.concatenate([owned * high, owned * low, owned], axis=0).astype(BF), ranked)
    ids = 32.0 * coded[0:NP] + coded[NP : 2 * NP] + coded[2 * NP :] - 1.0
    for p in range(NP):
        sids[p] = jnp.broadcast_to(ids[p : p + 1, :], (8, 128))
    loads[1].wait()
    packed = nn(pack_matrix(slot), h_ref[...]).astype(BF)
    sbuf[...] = packed.reshape(NP, CAP, D)
    rbuf[0] = packed[0:CAP]

    pl.semaphore_wait(barrier, NP - 1)
    copies = []
    for p in range(1, NP):
        peer = (me + p) % NP
        copies.append(remote(sids.at[p], rids.at[p], isend.at[p], irecv.at[p], geom, peer))
        copies.append(remote(sbuf.at[p], rbuf.at[p], send.at[p], recv.at[p], geom, peer))
    for copy in copies:
        copy.start()
    for load in loads[2:]:
        load.wait()
    for t in range(TILES):
        rows = slice(t * TE, (t + 1) * TE)
        src = src_ref[:, rows] - (me * C - HB)
        src_col = jnp.broadcast_to(src.astype(F32), (128, TE)).T.astype(jnp.int32)
        for b in range(PADDED // 128):
            sel_ref[rows, b * 128 : (b + 1) * 128] = (src_col == iota((TE, 128), 1) + b * 128).astype(BF)
        self_ref[rows, :] = nn(edges[rows, :], w_self[...]).astype(BF)
    for copy in copies[0::2]:
        copy.wait_recv()
    got = jnp.concatenate([ids[0:1]] + [rids[p, 0:1, :] for p in range(1, NP)], axis=0)
    ids_ref[...] = got
    for p, block in enumerate(unpack_blocks(got)):
        mt[pl.ds(p * CAP, CAP), :] = block
    for copy in copies[1::2]:
        copy.wait_recv()
    nodes = tn(mt[...], rbuf[...].reshape(SLOTS, D)).astype(BF)
    edge_out[0] = nodes[0:HB]
    edge_out[1] = nodes[C - HB : C]
    to_prev = remote(edge_out.at[0], edge_in.at[1], hsend.at[0], hrecv.at[1], geom, (me + NP - 1) % NP)
    to_next = remote(edge_out.at[1], edge_in.at[0], hsend.at[1], hrecv.at[0], geom, (me + 1) % NP)
    to_prev.start()
    to_next.start()
    pad_ref[HB : HB + C, :] = nodes
    to_prev.wait_recv()
    to_next.wait_recv()
    pad_ref[0:HB, :] = edge_in[0]
    pad_ref[HB + C :, :] = edge_in[1]
    for copy in copies:
        copy.wait_send()
    to_prev.wait_send()
    to_next.wait_send()


def deliver(h, tgt, source, edges, wei):
    vm = pl.BlockSpec(memory_space=pltpu.VMEM)
    hbm = pl.BlockSpec(memory_space=pltpu.HBM)
    return pl.pallas_call(
        deliver_kernel,
        out_shape=(
            jax.ShapeDtypeStruct((PADDED, D), BF),
            jax.ShapeDtypeStruct((NP, 128), F32),
            jax.ShapeDtypeStruct((1, C), jnp.int32),
            jax.ShapeDtypeStruct((C * K, PADDED), BF),
            jax.ShapeDtypeStruct((C * K, D), BF),
        ),
        in_specs=[hbm] * 5,
        out_specs=(vm,) * 5,
        scratch_shapes=[
            pltpu.VMEM((C, D), BF),
            pltpu.VMEM((1, C), jnp.int32),
            pltpu.VMEM((1, C * K), jnp.int32),
            pltpu.VMEM((C * K, D), BF),
            pltpu.VMEM((D, D), BF),
            pltpu.VMEM((NP, CAP, D), BF),
            pltpu.VMEM((NP, CAP, D), BF),
            pltpu.VMEM((NP, 8, 128), F32),
            pltpu.VMEM((NP, 8, 128), F32),
            pltpu.VMEM((2, HB, D), BF),
            pltpu.VMEM((2, HB, D), BF),
            pltpu.VMEM((SLOTS, C), BF),
        ]
        + [pltpu.SemaphoreType.DMA((NP,))] * 4
        + [pltpu.SemaphoreType.DMA((2,))] * 2
        + [pltpu.SemaphoreType.DMA((5,))],
        compiler_params=pltpu.CompilerParams(
            collective_id=0, has_side_effects=True, vmem_limit_bytes=18 * 1024 * 1024
        ),
        cost_estimate=pl.CostEstimate(flops=20_000_000_000, bytes_accessed=60_000_000, transcendentals=0),
        name="deliver",
    )(*(pltpu.with_memory_space_constraint(a, pltpu.HBM) for a in (h, tgt, source, edges, wei)))


def layer_kernel(
    pad_ref, src_ref, sel_ref, self_ref, edges_ref, cotn_ref, cote_ref, wei_ref, weo_ref, wni_ref, wno_ref,
    edge_new_ref, node_new_ref, grad_edge_ref, ng_ref, halo_ref,
    hid, post_grad, pre_grad, summed_ref, node_hid_ref, node_pre_ref, node_post_ref, recv_ref, send_ref,
    spread, four, comb, big, slope, normed, inv, ups, total,
):
    step = pl.program_id(0)
    me = lax.axis_index("dom")
    w_self, w_send, w_recv = wei_ref.at[0:D], wei_ref.at[D : 2 * D], wei_ref.at[2 * D : 3 * D]
    w_nself, w_nagg = wni_ref.at[0:D], wni_ref.at[D : 2 * D]
    rows = pl.ds(pl.multiple_of(step * TC, TC), TC)

    @pl.when(step == 0)
    def _():
        comb[0:PADDED, :] = nn(pad_ref[...], w_send[...]).astype(BF)
        spread[...] = (iota((TE, TC), 0) // K == iota((TE, TC), 1)).astype(BF)
        four[...] = (iota((TC, TE), 1) // K == iota((TC, TE), 0)).astype(BF)
        total[...] = jnp.zeros_like(total)

    nodes = pad_ref[pl.ds(pl.multiple_of(HB + step * TC, HB), TC), :]
    comb[PADDED:, :] = nn(nodes, w_recv[...]).astype(BF)

    big[...] = self_ref[...].astype(F32) + nn(jnp.concatenate([sel_ref[...], spread[...]], axis=1), comb[...])
    for r in range(0, TE, RC):
        v = big[r : r + RC, :]
        s = sigmoid(v)
        h = v * s
        hid[r : r + RC, :] = h.astype(BF)
        slope[r : r + RC, :] = s + h * (1.0 - s)
    big[...] = nn(hid[...], weo_ref[...])
    for r in range(0, TE, RC):
        v = big[r : r + RC, :]
        center = v - jnp.mean(v, axis=-1, keepdims=True)
        i = lax.rsqrt(jnp.mean(center * center, axis=-1, keepdims=True) + 1e-05)
        n = center * i
        normed[r : r + RC, :] = n
        inv[r : r + RC, :] = jnp.broadcast_to(i, (RC, 128))
        edge_new_ref[r : r + RC, :] = (edges_ref[r : r + RC, :].astype(F32) + n).astype(BF)

    summed = nn(four[...], edge_new_ref[...]).astype(BF)
    summed_ref[...] = summed
    v = nn(jnp.concatenate([nodes, summed], axis=1), wni_ref[...])
    s = sigmoid(v)
    h = v * s
    node_slope = s + h * (1.0 - s)
    node_hid = h.astype(BF)
    node_hid_ref[...] = node_hid
    v = nn(node_hid, wno_ref[...])
    center = v - jnp.mean(v, axis=-1, keepdims=True)
    i = lax.rsqrt(jnp.mean(center * center, axis=-1, keepdims=True) + 1e-05)
    n = center * i
    node_new_ref[...] = (nodes.astype(F32) + n).astype(BF)
    u = cotn_ref[...].astype(F32)
    m1 = jnp.mean(u, axis=-1, keepdims=True)
    m2 = jnp.mean(u * n, axis=-1, keepdims=True)
    node_post_grad = (i * (u - m1 - n * m2)).astype(BF)
    node_post_ref[...] = node_post_grad
    node_pre_grad = (nt(node_post_grad, wno_ref[...]) * node_slope).astype(BF)
    node_pre_ref[...] = node_pre_grad
    spread_grad = nt(node_pre_grad, w_nagg[...]).astype(BF)

    ups[...] = nn(spread[...], spread_grad)
    for r in range(0, TE, RC):
        u = cote_ref[r : r + RC, :].astype(F32) + ups[r : r + RC, :]
        ups[r : r + RC, :] = u
        n = normed[r : r + RC, :]
        m1 = jnp.mean(u, axis=-1, keepdims=True)
        m2 = jnp.mean(u * n, axis=-1, keepdims=True)
        post_grad[r : r + RC, :] = (inv[r : r + RC, 0:1] * (u - m1 - n * m2)).astype(BF)
    big[...] = nt(post_grad[...], weo_ref[...])
    for r in range(0, TE, RC):
        pre_grad[r : r + RC, :] = (big[r : r + RC, :] * slope[r : r + RC, :]).astype(BF)
    g = pre_grad[...]
    big[...] = nt(g, w_self[...])
    for r in range(0, TE, RC):
        grad_edge_ref[r : r + RC, :] = (ups[r : r + RC, :] + big[r : r + RC, :]).astype(BF)
    src = src_ref[...] - (me * C - HB)
    sel_t = (iota((PADDED, TE), 0) == src).astype(BF)
    gathered = nn(jnp.concatenate([sel_t, four[...]], axis=0), g)
    total[...] += gathered[0:PADDED]
    recv_grad = gathered[PADDED:].astype(BF)
    recv_ref[...] = recv_grad
    ng_ref[rows, :] = (
        cotn_ref[...].astype(F32) + nt(node_pre_grad, w_nself[...]) + nt(recv_grad, w_recv[...])
    )

    @pl.when(step == TILES - 1)
    def _():
        t = total[...].astype(BF)
        send_ref[...] = t
        back = nt(t, w_send[...])
        ng_ref[...] += back[HB : HB + C]
        halo_ref[0] = back[0:HB].astype(BF)
        halo_ref[1] = back[HB + C :].astype(BF)


def layer(padded, source, sel, pre_self, edges, cot_nodes, cot_edges, wei, weo, wni, wno):
    def whole(shape):
        return pl.BlockSpec(shape, lambda i: (0,) * len(shape), pipeline_mode=pl.Buffered(1))

    def tile(rows):
        return pl.BlockSpec((rows, D), lambda i: (i, 0))

    by_edge = jax.ShapeDtypeStruct((C * K, D), BF)
    by_cell = jax.ShapeDtypeStruct((C, D), BF)
    return pl.pallas_call(
        layer_kernel,
        grid=(TILES,),
        out_shape=(
            by_edge, by_cell, by_edge,
            jax.ShapeDtypeStruct((C, D), F32),
            jax.ShapeDtypeStruct((2, HB, D), BF),
            by_edge, by_edge, by_edge, by_cell, by_cell, by_cell, by_cell, by_cell,
            jax.ShapeDtypeStruct((PADDED, D), BF),
        ),
        in_specs=[
            whole((PADDED, D)),
            pl.BlockSpec((1, TE), lambda i: (0, i)),
            pl.BlockSpec((TE, PADDED), lambda i: (i, 0)),
            tile(TE),
            tile(TE), tile(TC), tile(TE),
            whole((3 * D, D)), whole((D, D)), whole((2 * D, D)), whole((D, D)),
        ],
        out_specs=(
            tile(TE), tile(TC), tile(TE),
            whole((C, D)), whole((2, HB, D)),
            tile(TE), tile(TE), tile(TE), tile(TC), tile(TC), tile(TC), tile(TC), tile(TC),
            whole((PADDED, D)),
        ),
        scratch_shapes=[
            pltpu.VMEM((TE, TC), BF),
            pltpu.VMEM((TC, TE), BF),
            pltpu.VMEM((SEL, D), BF),
            pltpu.VMEM((TE, D), F32),
            pltpu.VMEM((TE, D), F32),
            pltpu.VMEM((TE, D), F32),
            pltpu.VMEM((TE, 128), F32),
            pltpu.VMEM((TE, D), F32),
            pltpu.VMEM((PADDED, D), F32),
        ],
        compiler_params=pltpu.CompilerParams(vmem_limit_bytes=30 * 1024 * 1024),
        cost_estimate=pl.CostEstimate(flops=20_000_000_000, bytes_accessed=40_000_000, transcendentals=4_000_000),
        name="layer",
    )(padded, source, sel, pre_self, edges, cot_nodes, cot_edges, wei, weo, wni, wno)


ROWS = SQUARES * D
QW = 128
CW = 2 * QW
EARLY = 10
PART = 64
STARTS = (0, 64, 128, 160)


def collect_kernel(
    ng_ref, halo_ref, ids_ref,
    edges, pad, hid, post, pre, summed, nhid, npre, npost, recv_g, send_g,
    back_ref, fin_ref,
    hbuf, sback, rback, wown, wsend, pbuf, wsum, r1, p1, r2, r3, fin, wx, rx, px, ri, ag,
    hsend, hrecv, bsend, brecv, psend, precv, s1, v1, s2, v2, s3, v3, s4, v4, sx, vx, si, vi, sg, vg,
):
    geom = lax.axis_index("geom")
    me = lax.axis_index("dom")
    core = geom % 2
    x = geom // 2
    y = me // 4
    z = me % 4
    partner = x * 2 + (1 - core)
    i_me = y * (1 - core) + z * core
    j_me = z * (1 - core) + y * core

    def dom_of(i, j):
        return (i * 4 + j) * (1 - core) + (j * 4 + i) * core

    barrier = pltpu.get_barrier_semaphore()
    signals = NP - 1
    for p in range(1, NP):
        signal(barrier, geom, (me + p) % NP)
    for d in range(1, 8):
        signal(barrier, (geom + d) % 8, me)
        signals += 1

    scale = 1.0 / math.sqrt(8 * NP * C * K)
    inner = slice(HB, HB + C)
    operands = {
        0: (edges, None, pre), 1: (pad, None, send_g), 2: (pad, inner, recv_g), 3: (hid, None, post),
        4: (pad, inner, npre), 5: (summed, None, npre), 6: (nhid, None, npost),
    }
    pair = {}

    def square(q):
        left, cut, right = operands[q]
        rows = left[...] if cut is None else left[cut, :]
        value = (tn(rows, right[...]) * scale).astype(BF)
        for c in range(2):
            low, high = value[:, c * CW : c * CW + QW], value[:, c * CW + QW : (c + 1) * CW]
            wown[c, q] = jnp.where(core == 0, low, high)
            wsend[c, q] = jnp.where(core == 0, high, low)
            n = c * SQUARES + q
            pair[c, q] = remote(wsend.at[c, q], pbuf.at[c, q], psend.at[n], precv.at[n], partner, me)

    def reduced_block(c, k):
        parts = []
        at, end = k * PER_DOM, (k + 1) * PER_DOM
        while at < end:
            q, r = divmod(at, D)
            n = min(end - at, D - r)
            parts.append(wown[c, q, r : r + n].astype(F32) + pbuf[c, q, r : r + n].astype(F32))
            at += n
        value = parts[0] if len(parts) == 1 else jnp.concatenate(parts, axis=0)
        return value.astype(BF)

    seen = set()

    def joined(c, squares):
        for q in squares:
            if (c, q) not in seen:
                seen.add((c, q))
                pair[c, q].wait_recv()

    ones, xs, ys = {}, [], []

    def join(c):
        joined(c, range(SQUARES))
        for k in range(NP):
            i = (k // 4) * (1 - core) + (k % 4) * core
            j = (k % 4) * (1 - core) + (k // 4) * core
            wsum[pl.ds(i * 4 + j, 1)] = reduced_block(c, k).reshape(1, PER_DOM, QW)
        for d in range(1, 4):
            to = (i_me + d) % 4
            ones[d] = remote(
                wsum.at[pl.ds(to * 4, 4)], r1.at[d - 1], s1.at[d - 1], v1.at[d - 1], geom, dom_of(to, j_me)
            )
            ones[d].start()

    def join_x(c, low, high, squares):
        joined(c, squares)
        for k in range(low, high):
            value = reduced_block(c, k)
            for n, r in enumerate(STARTS):
                wx[n, k] = value[r : r + PART]
        for d in range(1, 4):
            to = (x + d) % 4
            n = len(xs)
            xs.append(
                remote(
                    wx.at[to, low:high], rx.at[d - 1, low:high], sx.at[n], vx.at[n], to * 2 + core, me
                )
            )
            xs[-1].start()

    def narrow_x():
        for copy in xs:
            copy.wait_recv()
        own = wx[pl.ds(x, 1)].reshape(NP, PART, QW).astype(F32)
        for d in range(3):
            own += rx[d].astype(F32)
        px[...] = own.astype(BF)
        for d in range(1, NP):
            to = (me + d) % NP
            ys.append(remote(px.at[to], ri.at[d - 1], si.at[d - 1], vi.at[d - 1], geom, to))
            ys[-1].start()

    gathers = []

    def narrow_dom():
        for copy in ys:
            copy.wait_recv()
        own = px[pl.ds(me, 1)].reshape(PART, QW).astype(F32)
        for d in range(NP - 1):
            own += ri[d].astype(F32)
        ag[pl.ds(geom, 1)] = own.astype(BF).reshape(1, PART, QW)
        for d in range(1, 8):
            gathers.append(
                remote(ag.at[geom], ag.at[geom], sg.at[d - 1], vg.at[d - 1], (geom + d) % 8, me)
            )
            gathers[-1].start()

    twos, threes = {}, {}

    def narrow():
        for d in range(1, 4):
            ones[d].wait_recv()
        for j in range(4):
            own = wsum[pl.ds(i_me * 4 + j, 1)].reshape(PER_DOM, QW).astype(F32)
            for d in range(3):
                own += r1[d, j].astype(F32)
            p1[j] = own.astype(BF)
        for d in range(1, 4):
            j = (j_me + d) % 4
            twos[d] = remote(p1.at[j], r2.at[d - 1], s2.at[d - 1], v2.at[d - 1], geom, dom_of(i_me, j))
            twos[d].start()

    def across():
        for d in range(1, 4):
            twos[d].wait_recv()
        own = p1[pl.ds(j_me, 1)].reshape(PER_DOM, QW).astype(F32)
        for d in range(3):
            own += r2[d].astype(F32)
        r3[pl.ds(x, 1)] = own.astype(BF).reshape(1, PER_DOM, QW)
        for d in range(1, 4):
            threes[d] = remote(r3.at[x], r3.at[x], s3.at[d - 1], v3.at[d - 1], ((x + d) % 4) * 2 + core, me)
            threes[d].start()

    def send_pairs(*squares):
        for c in (1, 0):
            for q in squares:
                pair[c, q].start()

    for q in (4, 5, 6):
        square(q)
    pl.semaphore_wait(barrier, signals)
    send_pairs(4, 5, 6)
    to_prev = remote(halo_ref.at[0], hbuf.at[1], hsend.at[0], hrecv.at[1], geom, (me + NP - 1) % NP)
    to_next = remote(halo_ref.at[1], hbuf.at[0], hsend.at[1], hrecv.at[0], geom, (me + 1) % NP)
    to_prev.start()
    to_next.start()
    square(3)
    send_pairs(3)
    join_x(1, EARLY, NP, (4, 5, 6))
    for q in (2, 1, 0):
        square(q)
        send_pairs(q)
    join_x(1, 0, EARLY, range(SQUARES))
    join(0)

    blocks = jnp.concatenate(unpack_blocks(ids_ref[...]), axis=0)
    to_prev.wait_recv()
    to_next.wait_recv()
    first = ng_ref[0:HB, :] + hbuf[0].astype(F32)
    last = ng_ref[C - HB :, :] + hbuf[1].astype(F32)
    cells = jnp.concatenate([first, ng_ref[HB : C - HB, :], last], axis=0).astype(BF)
    packed = nn(blocks, cells).astype(BF)
    sback[...] = packed.reshape(NP, CAP, D)
    rback[0] = packed[0:CAP]
    backs = [
        remote(sback.at[p], rback.at[p], bsend.at[p], brecv.at[p], geom, (me + NP - p) % NP)
        for p in range(1, NP)
    ]
    for copy in backs:
        copy.start()

    narrow_x()
    narrow()
    across()
    narrow_dom()
    for copy in backs:
        copy.wait_recv()
    back_ref[...] = rback[...].reshape(SLOTS, D)
    for d in range(1, 4):
        origin = (x + 4 - d) % 4
        remote(r3.at[x], r3.at[origin], s3.at[d - 1], v3.at[d - 1], origin * 2 + core, me).wait_recv()
    done = r3[0].astype(F32) + r3[1].astype(F32) + r3[2].astype(F32) + r3[3].astype(F32)
    fin[pl.ds(core, 1)] = done.astype(BF).reshape(1, PER_DOM, QW)
    four = remote(fin.at[core], fin.at[core], s4, v4, partner, me)
    four.start()
    for d in range(1, 8):
        origin = (geom + 8 - d) % 8
        remote(ag.at[geom], ag.at[origin], sg.at[d - 1], vg.at[d - 1], origin, me).wait_recv()
    for q in range(2):
        for n, r in enumerate(STARTS):
            fin_ref[r : r + PART, CW + q * QW : CW + (q + 1) * QW] = ag[n * 2 + q]
    remote(fin.at[core], fin.at[1 - core], s4, v4, partner, me).wait_recv()
    for q in range(2):
        fin_ref[:, q * QW : (q + 1) * QW] = fin[q]
    groups = (pair, ones, twos, threes)
    for copy in [to_prev, to_next, four] + backs + xs + ys + gathers:
        copy.wait_send()
    for group in groups:
        for copy in group.values():
            copy.wait_send()


def finish_kernel(back_ref, slot_ref, fin_ref, grad_ref, out_ref):
    grad_ref[...] = tn(pack_matrix(slot_ref[...]), back_ref[...]).astype(BF)
    out_ref[...] = fin_ref[...].astype(F32)


def finish(back, slot, fin):
    vm = pl.BlockSpec(memory_space=pltpu.VMEM)
    return pl.pallas_call(
        finish_kernel,
        out_shape=(jax.ShapeDtypeStruct((C, D), BF), jax.ShapeDtypeStruct((PER_DOM, D), F32)),
        in_specs=[vm] * 3,
        out_specs=(vm, vm),
        compiler_params=pltpu.CompilerParams(vmem_limit_bytes=8 * 1024 * 1024),
        name="finish",
    )(back, slot, fin)


def collect(ng, halo, ids, *operands):
    vm = pl.BlockSpec(memory_space=pltpu.VMEM)
    dma = pltpu.SemaphoreType.DMA
    return pl.pallas_call(
        collect_kernel,
        out_shape=(
            jax.ShapeDtypeStruct((SLOTS, D), BF),
            jax.ShapeDtypeStruct((PER_DOM, D), BF),
        ),
        in_specs=[vm] * (3 + len(operands)),
        out_specs=(vm, vm),
        scratch_shapes=[
            pltpu.VMEM((2, HB, D), BF),
            pltpu.VMEM((NP, CAP, D), BF),
            pltpu.VMEM((NP, CAP, D), BF),
            pltpu.VMEM((2, SQUARES, D, QW), BF),
            pltpu.VMEM((2, SQUARES, D, QW), BF),
            pltpu.VMEM((2, SQUARES, D, QW), BF),
            pltpu.VMEM((NP, PER_DOM, QW), BF),
            pltpu.VMEM((3, 4, PER_DOM, QW), BF),
            pltpu.VMEM((4, PER_DOM, QW), BF),
            pltpu.VMEM((3, PER_DOM, QW), BF),
            pltpu.VMEM((4, PER_DOM, QW), BF),
            pltpu.VMEM((2, PER_DOM, QW), BF),
            pltpu.VMEM((4, NP, PART, QW), BF),
            pltpu.VMEM((3, NP, PART, QW), BF),
            pltpu.VMEM((NP, PART, QW), BF),
            pltpu.VMEM((NP - 1, PART, QW), BF),
            pltpu.VMEM((8, PART, QW), BF),
            dma((2,)), dma((2,)), dma((NP,)), dma((NP,)),
            dma((2 * SQUARES,)), dma((2 * SQUARES,)), dma((3,)), dma((3,)),
            dma((3,)), dma((3,)), dma((3,)), dma((3,)), dma, dma,
            dma((6,)), dma((6,)), dma((NP - 1,)), dma((NP - 1,)), dma((7,)), dma((7,)),
        ],
        compiler_params=pltpu.CompilerParams(
            collective_id=1, has_side_effects=True, vmem_limit_bytes=32 * 1024 * 1024
        ),
        name="collect",
    )(ng, halo, ids, *operands)


def local(
    h_in, edge_in, new_index, source, w_edge_in, w_edge_out, w_node_in, w_node_out, cot_nodes, cot_edges
):
    padded, ids, slot, sel, pre_self = deliver(h_in[0], new_index, source, edge_in[0], w_edge_in)
    edge_new, node_new, grad_edge, ng, halo, hid, post, pre, summed, nhid, npre, npost, recv, send = layer(
        padded, source, sel, pre_self, edge_in[0], cot_nodes[0], cot_edges[0], w_edge_in, w_edge_out, w_node_in, w_node_out
    )
    back, fin = collect(
        ng, halo, ids, edge_in[0], padded, hid, post, pre, summed, nhid, npre, npost, recv, send
    )
    grad_in, weight_grads = finish(back, slot, fin)
    return (node_new[None], edge_new[None], grad_in[None], grad_edge[None], weight_grads)


def solution(mesh):
    return jax.shard_map(
        local,
        mesh=mesh,
        in_specs=(
            P("geom", "dom", None),
            P("geom", "dom", None),
            P("geom", "dom"),
            P("geom", "dom"),
            P(),
            P(),
            P(),
            P(),
            P("geom", "dom", None),
            P("geom", "dom", None),
        ),
        out_specs=(
            P("geom", "dom", None),
            P("geom", "dom", None),
            P("geom", "dom", None),
            P("geom", "dom", None),
            P("dom", None),
        ),
        check_vma=False,
    )
```

```python
import functools
import math

import jax
import jax.numpy as jnp
from jax import lax
from jax.experimental import pallas as pl
from jax.experimental.pallas import tpu as pltpu
from jax.sharding import PartitionSpec as P

MESH = pl.DeviceIdType.MESH
BF = jnp.bfloat16
F32 = jnp.float32

D = 512
K = 4
C = 512
HB = 64
PADDED = C + 2 * HB
NP = 16
CAP = 48
SLOTS = NP * CAP
TC = 128
TE = TC * K
TILES = C // TC
SEL = PADDED + TC
RC = 64
SQUARES = 7
PER_DOM = SQUARES * D // NP


def nn(a, b):
    return jnp.dot(a, b, preferred_element_type=F32)


def nt(a, b):
    return lax.dot_general(a, b, (((1,), (1,)), ((), ())), preferred_element_type=F32)


def tn(a, b):
    return lax.dot_general(a, b, (((0,), (0,)), ((), ())), preferred_element_type=F32)


def sigmoid(v):
    return 0.5 * jnp.tanh(0.5 * v) + 0.5


def iota(shape, dim):
    return lax.broadcasted_iota(jnp.int32, shape, dim)


def remote(src, dst, send, recv, geom, dom):
    return pltpu.make_async_remote_copy(
        src_ref=src,
        dst_ref=dst,
        send_sem=send,
        recv_sem=recv,
        device_id=(geom, dom),
        device_id_type=MESH,
    )


def signal(sem, geom, dom):
    pl.semaphore_signal(sem, inc=1, device_id=(geom, dom), device_id_type=MESH)


def pack_matrix(slot):
    return (iota((SLOTS, C), 0) == slot).astype(BF)


def unpack_blocks(ids):
    turned = ids.T
    lanes = iota((CAP, C), 1).astype(F32)
    return [(turned[0:CAP, p : p + 1] == lanes).astype(BF) for p in range(NP)]


def deliver_kernel(
    h_hbm, tgt_hbm, src_hbm, edges_hbm, w_hbm,
    pad_ref, ids_ref, slot_ref, sel_ref, self_ref,
    h_ref, tgt_ref, src_ref, edges, w_self, sbuf, rbuf, sids, rids, edge_out, edge_in, mt,
    send, recv, isend, irecv, hsend, hrecv, lsem,
):
    geom = lax.axis_index("geom")
    me = lax.axis_index("dom")
    barrier = pltpu.get_barrier_semaphore()
    for p in range(1, NP):
        signal(barrier, geom, (me + p) % NP)

    loads = [
        pltpu.make_async_copy(far, near, lsem.at[n])
        for n, (far, near) in enumerate(
            ((tgt_hbm, tgt_ref), (h_hbm, h_ref), (edges_hbm, edges), (w_hbm.at[0:D], w_self), (src_hbm, src_ref))
        )
    ]
    for load in loads:
        load.start()
    loads[0].wait()
    tgt = tgt_ref[...]
    off = ((tgt >> 9) - me) & (NP - 1)
    row = tgt & (C - 1)
    owned = (iota((NP, C), 0) == off).astype(F32)
    upper = (iota((C, C), 0) < iota((C, C), 1)).astype(BF)
    before = nn(owned.astype(BF), upper)
    rank = jnp.sum(owned * before, axis=0, keepdims=True).astype(jnp.int32)
    slot = off * CAP + rank
    slot_ref[...] = slot
    ranked = (iota((128, C), 0) == rank).astype(BF)
    high = (row >> 5).astype(F32)
    low = (row & 31).astype(F32)
    coded = nt(jnp.concatenate([owned * high, owned * low, owned], axis=0).astype(BF), ranked)
    ids = 32.0 * coded[0:NP] + coded[NP : 2 * NP] + coded[2 * NP :] - 1.0
    for p in range(NP):
        sids[p] = jnp.broadcast_to(ids[p : p + 1, :], (8, 128))
    loads[1].wait()
    packed = nn(pack_matrix(slot), h_ref[...]).astype(BF)
    sbuf[...] = packed.reshape(NP, CAP, D)
    rbuf[0] = packed[0:CAP]

    pl.semaphore_wait(barrier, NP - 1)
    copies = []
    for p in range(1, NP):
        peer = (me + p) % NP
        copies.append(remote(sids.at[p], rids.at[p], isend.at[p], irecv.at[p], geom, peer))
        copies.append(remote(sbuf.at[p], rbuf.at[p], send.at[p], recv.at[p], geom, peer))
    for copy in copies:
        copy.start()
    for load in loads[2:]:
        load.wait()
    for t in range(TILES):
        rows = slice(t * TE, (t + 1) * TE)
        src = src_ref[:, rows] - (me * C - HB)
        src_col = jnp.broadcast_to(src.astype(F32), (128, TE)).T.astype(jnp.int32)
        for b in range(PADDED // 128):
            sel_ref[rows, b * 128 : (b + 1) * 128] = (src_col == iota((TE, 128), 1) + b * 128).astype(BF)
        self_ref[rows, :] = nn(edges[rows, :], w_self[...]).astype(BF)
    for copy in copies[0::2]:
        copy.wait_recv()
    got = jnp.concatenate([ids[0:1]] + [rids[p, 0:1, :] for p in range(1, NP)], axis=0)
    ids_ref[...] = got
    for p, block in enumerate(unpack_blocks(got)):
        mt[pl.ds(p * CAP, CAP), :] = block
    for copy in copies[1::2]:
        copy.wait_recv()
    nodes = tn(mt[...], rbuf[...].reshape(SLOTS, D)).astype(BF)
    edge_out[0] = nodes[0:HB]
    edge_out[1] = nodes[C - HB : C]
    to_prev = remote(edge_out.at[0], edge_in.at[1], hsend.at[0], hrecv.at[1], geom, (me + NP - 1) % NP)
    to_next = remote(edge_out.at[1], edge_in.at[0], hsend.at[1], hrecv.at[0], geom, (me + 1) % NP)
    to_prev.start()
    to_next.start()
    pad_ref[HB : HB + C, :] = nodes
    to_prev.wait_recv()
    to_next.wait_recv()
    pad_ref[0:HB, :] = edge_in[0]
    pad_ref[HB + C :, :] = edge_in[1]
    for copy in copies:
        copy.wait_send()
    to_prev.wait_send()
    to_next.wait_send()


def deliver(h, tgt, source, edges, wei):
    vm = pl.BlockSpec(memory_space=pltpu.VMEM)
    hbm = pl.BlockSpec(memory_space=pltpu.HBM)
    return pl.pallas_call(
        deliver_kernel,
        out_shape=(
            jax.ShapeDtypeStruct((PADDED, D), BF),
            jax.ShapeDtypeStruct((NP, 128), F32),
            jax.ShapeDtypeStruct((1, C), jnp.int32),
            jax.ShapeDtypeStruct((C * K, PADDED), BF),
            jax.ShapeDtypeStruct((C * K, D), BF),
        ),
        in_specs=[hbm] * 5,
        out_specs=(vm,) * 5,
        scratch_shapes=[
            pltpu.VMEM((C, D), BF),
            pltpu.VMEM((1, C), jnp.int32),
            pltpu.VMEM((1, C * K), jnp.int32),
            pltpu.VMEM((C * K, D), BF),
            pltpu.VMEM((D, D), BF),
            pltpu.VMEM((NP, CAP, D), BF),
            pltpu.VMEM((NP, CAP, D), BF),
            pltpu.VMEM((NP, 8, 128), F32),
            pltpu.VMEM((NP, 8, 128), F32),
            pltpu.VMEM((2, HB, D), BF),
            pltpu.VMEM((2, HB, D), BF),
            pltpu.VMEM((SLOTS, C), BF),
        ]
        + [pltpu.SemaphoreType.DMA((NP,))] * 4
        + [pltpu.SemaphoreType.DMA((2,))] * 2
        + [pltpu.SemaphoreType.DMA((5,))],
        compiler_params=pltpu.CompilerParams(
            collective_id=0, has_side_effects=True, vmem_limit_bytes=18 * 1024 * 1024
        ),
        cost_estimate=pl.CostEstimate(flops=20_000_000_000, bytes_accessed=60_000_000, transcendentals=0),
        name="deliver",
    )(*(pltpu.with_memory_space_constraint(a, pltpu.HBM) for a in (h, tgt, source, edges, wei)))


def layer_kernel(
    pad_ref, src_all, sel_all, self_all, edges_all, cotn_all, cote_all, wei_ref, weo_ref, wni_ref, wno_ref,
    edge_new_ref, node_new_ref, grad_edge_ref, ng_ref, halo_ref,
    hid_all, post_all, pre_all, summed_all, node_hid_all, node_pre_all, node_post_all, recv_all, send_ref,
    spread, four, comb, big, slope, normed, inv, ups, total,
):
    step = pl.program_id(0)
    me = lax.axis_index("dom")
    w_self, w_send, w_recv = wei_ref.at[0:D], wei_ref.at[D : 2 * D], wei_ref.at[2 * D : 3 * D]
    w_nself, w_nagg = wni_ref.at[0:D], wni_ref.at[D : 2 * D]
    rows = pl.ds(pl.multiple_of(step * TC, TC), TC)
    lines = pl.ds(pl.multiple_of(step * TE, TE), TE)
    sel_ref, self_ref, edges_ref, cote_ref = (ref.at[lines] for ref in (sel_all, self_all, edges_all, cote_all))
    hid, post_grad, pre_grad = (ref.at[lines] for ref in (hid_all, post_all, pre_all))
    cotn_ref, summed_ref, node_hid_ref, node_pre_ref, node_post_ref, recv_ref = (
        ref.at[rows] for ref in (cotn_all, summed_all, node_hid_all, node_pre_all, node_post_all, recv_all)
    )

    @pl.when(step == 0)
    def _():
        comb[0:PADDED, :] = nn(pad_ref[...], w_send[...]).astype(BF)
        spread[...] = (iota((TE, TC), 0) // K == iota((TE, TC), 1)).astype(BF)
        four[...] = (iota((TC, TE), 1) // K == iota((TC, TE), 0)).astype(BF)
        total[...] = jnp.zeros_like(total)

    nodes = pad_ref[pl.ds(pl.multiple_of(HB + step * TC, HB), TC), :]
    comb[PADDED:, :] = nn(nodes, w_recv[...]).astype(BF)

    big[...] = self_ref[...].astype(F32) + nn(jnp.concatenate([sel_ref[...], spread[...]], axis=1), comb[...])
    for r in range(0, TE, RC):
        v = big[r : r + RC, :]
        s = sigmoid(v)
        h = v * s
        hid[r : r + RC, :] = h.astype(BF)
        slope[r : r + RC, :] = s + h * (1.0 - s)
    big[...] = nn(hid[...], weo_ref[...])
    for r in range(0, TE, RC):
        v = big[r : r + RC, :]
        center = v - jnp.mean(v, axis=-1, keepdims=True)
        i = lax.rsqrt(jnp.mean(center * center, axis=-1, keepdims=True) + 1e-05)
        n = center * i
        normed[r : r + RC, :] = n
        inv[r : r + RC, :] = jnp.broadcast_to(i, (RC, 128))
        edge_new_ref[r : r + RC, :] = (edges_ref[r : r + RC, :].astype(F32) + n).astype(BF)

    summed = nn(four[...], edge_new_ref[...]).astype(BF)
    summed_ref[...] = summed
    v = nn(jnp.concatenate([nodes, summed], axis=1), wni_ref[...])
    s = sigmoid(v)
    h = v * s
    node_slope = s + h * (1.0 - s)
    node_hid = h.astype(BF)
    node_hid_ref[...] = node_hid
    v = nn(node_hid, wno_ref[...])
    center = v - jnp.mean(v, axis=-1, keepdims=True)
    i = lax.rsqrt(jnp.mean(center * center, axis=-1, keepdims=True) + 1e-05)
    n = center * i
    node_new_ref[...] = (nodes.astype(F32) + n).astype(BF)
    u = cotn_ref[...].astype(F32)
    m1 = jnp.mean(u, axis=-1, keepdims=True)
    m2 = jnp.mean(u * n, axis=-1, keepdims=True)
    node_post_grad = (i * (u - m1 - n * m2)).astype(BF)
    node_post_ref[...] = node_post_grad
    node_pre_grad = (nt(node_post_grad, wno_ref[...]) * node_slope).astype(BF)
    node_pre_ref[...] = node_pre_grad
    spread_grad = nt(node_pre_grad, w_nagg[...]).astype(BF)

    ups[...] = nn(spread[...], spread_grad)
    for r in range(0, TE, RC):
        u = cote_ref[r : r + RC, :].astype(F32) + ups[r : r + RC, :]
        ups[r : r + RC, :] = u
        n = normed[r : r + RC, :]
        m1 = jnp.mean(u, axis=-1, keepdims=True)
        m2 = jnp.mean(u * n, axis=-1, keepdims=True)
        post_grad[r : r + RC, :] = (inv[r : r + RC, 0:1] * (u - m1 - n * m2)).astype(BF)
    big[...] = nt(post_grad[...], weo_ref[...])
    for r in range(0, TE, RC):
        pre_grad[r : r + RC, :] = (big[r : r + RC, :] * slope[r : r + RC, :]).astype(BF)
    g = pre_grad[...]
    big[...] = nt(g, w_self[...])
    for r in range(0, TE, RC):
        grad_edge_ref[r : r + RC, :] = (ups[r : r + RC, :] + big[r : r + RC, :]).astype(BF)
    src = src_all[:, lines] - (me * C - HB)
    sel_t = (iota((PADDED, TE), 0) == src).astype(BF)
    gathered = nn(jnp.concatenate([sel_t, four[...]], axis=0), g)
    total[...] += gathered[0:PADDED]
    recv_grad = gathered[PADDED:].astype(BF)
    recv_ref[...] = recv_grad
    ng_ref[rows, :] = (
        cotn_ref[...].astype(F32) + nt(node_pre_grad, w_nself[...]) + nt(recv_grad, w_recv[...])
    )

    @pl.when(step == TILES - 1)
    def _():
        t = total[...].astype(BF)
        send_ref[...] = t
        back = nt(t, w_send[...])
        ng_ref[...] += back[HB : HB + C]
        halo_ref[0] = back[0:HB].astype(BF)
        halo_ref[1] = back[HB + C :].astype(BF)


def layer(padded, source, sel, pre_self, edges, cot_nodes, cot_edges, wei, weo, wni, wno):
    vm = pl.BlockSpec(memory_space=pltpu.VMEM)

    def tile(rows):
        return pl.BlockSpec((rows, D), lambda i: (i, 0))

    by_edge = jax.ShapeDtypeStruct((C * K, D), BF)
    by_cell = jax.ShapeDtypeStruct((C, D), BF)
    return pl.pallas_call(
        layer_kernel,
        grid=(TILES,),
        out_shape=(
            by_edge, by_cell, by_edge,
            jax.ShapeDtypeStruct((C, D), F32),
            jax.ShapeDtypeStruct((2, HB, D), BF),
            by_edge, by_edge, by_edge, by_cell, by_cell, by_cell, by_cell, by_cell,
            jax.ShapeDtypeStruct((PADDED, D), BF),
        ),
        in_specs=[vm] * 11,
        out_specs=(tile(TE), tile(TC), tile(TE)) + (vm,) * 11,
        scratch_shapes=[
            pltpu.VMEM((TE, TC), BF),
            pltpu.VMEM((TC, TE), BF),
            pltpu.VMEM((SEL, D), BF),
            pltpu.VMEM((TE, D), F32),
            pltpu.VMEM((TE, D), F32),
            pltpu.VMEM((TE, D), F32),
            pltpu.VMEM((TE, 128), F32),
            pltpu.VMEM((TE, D), F32),
            pltpu.VMEM((PADDED, D), F32),
        ],
        compiler_params=pltpu.CompilerParams(vmem_limit_bytes=30 * 1024 * 1024),
        cost_estimate=pl.CostEstimate(flops=20_000_000_000, bytes_accessed=40_000_000, transcendentals=4_000_000),
        name="layer",
    )(padded, source, sel, pre_self, edges, cot_nodes, cot_edges, wei, weo, wni, wno)


ROWS = SQUARES * D
QW = 128
CW = 2 * QW
EARLY = 10
PART = 64
STARTS = (0, 64, 128, 160)


def collect_kernel(
    ng_ref, halo_ref, ids_ref,
    edges, pad, hid, post, pre, summed, nhid, npre, npost, recv_g, send_g,
    back_ref, fin_ref,
    hbuf, sback, rback, wown, wsend, pbuf, wsum, r1, p1, r2, r3, fin, wx, rx, px, ri, ag,
    hsend, hrecv, bsend, brecv, psend, precv, s1, v1, s2, v2, s3, v3, s4, v4, sx, vx, si, vi, sg, vg,
):
    geom = lax.axis_index("geom")
    me = lax.axis_index("dom")
    core = geom % 2
    x = geom // 2
    y = me // 4
    z = me % 4
    partner = x * 2 + (1 - core)
    i_me = y * (1 - core) + z * core
    j_me = z * (1 - core) + y * core

    def dom_of(i, j):
        return (i * 4 + j) * (1 - core) + (j * 4 + i) * core

    barrier = pltpu.get_barrier_semaphore()
    signals = NP - 1
    for p in range(1, NP):
        signal(barrier, geom, (me + p) % NP)
    for d in range(1, 8):
        signal(barrier, (geom + d) % 8, me)
        signals += 1

    scale = 1.0 / math.sqrt(8 * NP * C * K)
    inner = slice(HB, HB + C)
    operands = {
        0: (edges, None, pre), 1: (pad, None, send_g), 2: (pad, inner, recv_g), 3: (hid, None, post),
        4: (pad, inner, npre), 5: (summed, None, npre), 6: (nhid, None, npost),
    }
    pair = {}

    def square(q):
        left, cut, right = operands[q]
        rows = left[...] if cut is None else left[cut, :]
        value = (tn(rows, right[...]) * scale).astype(BF)
        for c in range(2):
            low, high = value[:, c * CW : c * CW + QW], value[:, c * CW + QW : (c + 1) * CW]
            wown[c, q] = jnp.where(core == 0, low, high)
            wsend[c, q] = jnp.where(core == 0, high, low)
            n = c * SQUARES + q
            pair[c, q] = remote(wsend.at[c, q], pbuf.at[c, q], psend.at[n], precv.at[n], partner, me)

    def reduced_block(c, k):
        parts = []
        at, end = k * PER_DOM, (k + 1) * PER_DOM
        while at < end:
            q, r = divmod(at, D)
            n = min(end - at, D - r)
            parts.append(wown[c, q, r : r + n].astype(F32) + pbuf[c, q, r : r + n].astype(F32))
            at += n
        value = parts[0] if len(parts) == 1 else jnp.concatenate(parts, axis=0)
        return value.astype(BF)

    seen = set()

    def joined(c, squares):
        for q in squares:
            if (c, q) not in seen:
                seen.add((c, q))
                pair[c, q].wait_recv()

    ones, xs, ys = {}, [], []

    def join(c):
        joined(c, range(SQUARES))
        for k in range(NP):
            i = (k // 4) * (1 - core) + (k % 4) * core
            j = (k % 4) * (1 - core) + (k // 4) * core
            wsum[pl.ds(i * 4 + j, 1)] = reduced_block(c, k).reshape(1, PER_DOM, QW)
        for d in range(1, 4):
            to = (i_me + d) % 4
            ones[d] = remote(
                wsum.at[pl.ds(to * 4, 4)], r1.at[d - 1], s1.at[d - 1], v1.at[d - 1], geom, dom_of(to, j_me)
            )
            ones[d].start()

    def join_x(c, low, high, squares):
        joined(c, squares)
        for k in range(low, high):
            value = reduced_block(c, k)
            for n, r in enumerate(STARTS):
                wx[n, k] = value[r : r + PART]
        for d in range(1, 4):
            to = (x + d) % 4
            n = len(xs)
            xs.append(
                remote(
                    wx.at[to, low:high], rx.at[d - 1, low:high], sx.at[n], vx.at[n], to * 2 + core, me
                )
            )
            xs[-1].start()

    def narrow_x():
        for copy in xs:
            copy.wait_recv()
        own = wx[pl.ds(x, 1)].reshape(NP, PART, QW).astype(F32)
        for d in range(3):
            own += rx[d].astype(F32)
        px[...] = own.astype(BF)
        for d in range(1, NP):
            to = (me + d) % NP
            ys.append(remote(px.at[to], ri.at[d - 1], si.at[d - 1], vi.at[d - 1], geom, to))
            ys[-1].start()

    gathers = []

    def narrow_dom():
        for copy in ys:
            copy.wait_recv()
        own = px[pl.ds(me, 1)].reshape(PART, QW).astype(F32)
        for d in range(NP - 1):
            own += ri[d].astype(F32)
        ag[pl.ds(geom, 1)] = own.astype(BF).reshape(1, PART, QW)
        for d in range(1, 8):
            gathers.append(
                remote(ag.at[geom], ag.at[geom], sg.at[d - 1], vg.at[d - 1], (geom + d) % 8, me)
            )
            gathers[-1].start()

    twos, threes = {}, {}

    def narrow():
        for d in range(1, 4):
            ones[d].wait_recv()
        for j in range(4):
            own = wsum[pl.ds(i_me * 4 + j, 1)].reshape(PER_DOM, QW).astype(F32)
            for d in range(3):
                own += r1[d, j].astype(F32)
            p1[j] = own.astype(BF)
        for d in range(1, 4):
            j = (j_me + d) % 4
            twos[d] = remote(p1.at[j], r2.at[d - 1], s2.at[d - 1], v2.at[d - 1], geom, dom_of(i_me, j))
            twos[d].start()

    def across():
        for d in range(1, 4):
            twos[d].wait_recv()
        own = p1[pl.ds(j_me, 1)].reshape(PER_DOM, QW).astype(F32)
        for d in range(3):
            own += r2[d].astype(F32)
        r3[pl.ds(x, 1)] = own.astype(BF).reshape(1, PER_DOM, QW)
        for d in range(1, 4):
            threes[d] = remote(r3.at[x], r3.at[x], s3.at[d - 1], v3.at[d - 1], ((x + d) % 4) * 2 + core, me)
            threes[d].start()

    def send_pairs(*squares):
        for c in (1, 0):
            for q in squares:
                pair[c, q].start()

    for q in (4, 5, 6, 3, 2, 1, 0):
        square(q)
    pl.semaphore_wait(barrier, signals)
    send_pairs(4, 5, 6)
    to_prev = remote(halo_ref.at[0], hbuf.at[1], hsend.at[0], hrecv.at[1], geom, (me + NP - 1) % NP)
    to_next = remote(halo_ref.at[1], hbuf.at[0], hsend.at[1], hrecv.at[0], geom, (me + 1) % NP)
    to_prev.start()
    to_next.start()
    send_pairs(3, 2, 1, 0)
    join_x(1, EARLY, NP, (4, 5, 6))
    join_x(1, 0, EARLY, range(SQUARES))
    join(0)

    blocks = jnp.concatenate(unpack_blocks(ids_ref[...]), axis=0)
    to_prev.wait_recv()
    to_next.wait_recv()
    first = ng_ref[0:HB, :] + hbuf[0].astype(F32)
    last = ng_ref[C - HB :, :] + hbuf[1].astype(F32)
    cells = jnp.concatenate([first, ng_ref[HB : C - HB, :], last], axis=0).astype(BF)
    packed = nn(blocks, cells).astype(BF)
    sback[...] = packed.reshape(NP, CAP, D)
    rback[0] = packed[0:CAP]
    backs = [
        remote(sback.at[p], rback.at[p], bsend.at[p], brecv.at[p], geom, (me + NP - p) % NP)
        for p in range(1, NP)
    ]
    for copy in backs:
        copy.start()

    narrow()
    narrow_x()
    across()
    narrow_dom()
    for copy in backs:
        copy.wait_recv()
    back_ref[...] = rback[...].reshape(SLOTS, D)
    for d in range(1, 4):
        origin = (x + 4 - d) % 4
        remote(r3.at[x], r3.at[origin], s3.at[d - 1], v3.at[d - 1], origin * 2 + core, me).wait_recv()
    done = r3[0].astype(F32) + r3[1].astype(F32) + r3[2].astype(F32) + r3[3].astype(F32)
    fin[pl.ds(core, 1)] = done.astype(BF).reshape(1, PER_DOM, QW)
    four = remote(fin.at[core], fin.at[core], s4, v4, partner, me)
    four.start()
    for d in range(1, 8):
        origin = (geom + 8 - d) % 8
        remote(ag.at[geom], ag.at[origin], sg.at[d - 1], vg.at[d - 1], origin, me).wait_recv()
    for q in range(2):
        for n, r in enumerate(STARTS):
            fin_ref[r : r + PART, CW + q * QW : CW + (q + 1) * QW] = ag[n * 2 + q]
    remote(fin.at[core], fin.at[1 - core], s4, v4, partner, me).wait_recv()
    for q in range(2):
        fin_ref[:, q * QW : (q + 1) * QW] = fin[q]
    groups = (pair, ones, twos, threes)
    for copy in [to_prev, to_next, four] + backs + xs + ys + gathers:
        copy.wait_send()
    for group in groups:
        for copy in group.values():
            copy.wait_send()


def finish_kernel(back_ref, slot_ref, fin_ref, grad_ref, out_ref):
    grad_ref[...] = tn(pack_matrix(slot_ref[...]), back_ref[...]).astype(BF)
    out_ref[...] = fin_ref[...].astype(F32)


def finish(back, slot, fin):
    vm = pl.BlockSpec(memory_space=pltpu.VMEM)
    return pl.pallas_call(
        finish_kernel,
        out_shape=(jax.ShapeDtypeStruct((C, D), BF), jax.ShapeDtypeStruct((PER_DOM, D), F32)),
        in_specs=[vm] * 3,
        out_specs=(vm, vm),
        compiler_params=pltpu.CompilerParams(vmem_limit_bytes=8 * 1024 * 1024),
        name="finish",
    )(back, slot, fin)


def collect(ng, halo, ids, *operands):
    vm = pl.BlockSpec(memory_space=pltpu.VMEM)
    dma = pltpu.SemaphoreType.DMA
    return pl.pallas_call(
        collect_kernel,
        out_shape=(
            jax.ShapeDtypeStruct((SLOTS, D), BF),
            jax.ShapeDtypeStruct((PER_DOM, D), BF),
        ),
        in_specs=[vm] * (3 + len(operands)),
        out_specs=(vm, vm),
        scratch_shapes=[
            pltpu.VMEM((2, HB, D), BF),
            pltpu.VMEM((NP, CAP, D), BF),
            pltpu.VMEM((NP, CAP, D), BF),
            pltpu.VMEM((2, SQUARES, D, QW), BF),
            pltpu.VMEM((2, SQUARES, D, QW), BF),
            pltpu.VMEM((2, SQUARES, D, QW), BF),
            pltpu.VMEM((NP, PER_DOM, QW), BF),
            pltpu.VMEM((3, 4, PER_DOM, QW), BF),
            pltpu.VMEM((4, PER_DOM, QW), BF),
            pltpu.VMEM((3, PER_DOM, QW), BF),
            pltpu.VMEM((4, PER_DOM, QW), BF),
            pltpu.VMEM((2, PER_DOM, QW), BF),
            pltpu.VMEM((4, NP, PART, QW), BF),
            pltpu.VMEM((3, NP, PART, QW), BF),
            pltpu.VMEM((NP, PART, QW), BF),
            pltpu.VMEM((NP - 1, PART, QW), BF),
            pltpu.VMEM((8, PART, QW), BF),
            dma((2,)), dma((2,)), dma((NP,)), dma((NP,)),
            dma((2 * SQUARES,)), dma((2 * SQUARES,)), dma((3,)), dma((3,)),
            dma((3,)), dma((3,)), dma((3,)), dma((3,)), dma, dma,
            dma((6,)), dma((6,)), dma((NP - 1,)), dma((NP - 1,)), dma((7,)), dma((7,)),
        ],
        compiler_params=pltpu.CompilerParams(
            collective_id=1, has_side_effects=True, vmem_limit_bytes=32 * 1024 * 1024
        ),
        name="collect",
    )(ng, halo, ids, *operands)


def local(
    h_in, edge_in, new_index, source, w_edge_in, w_edge_out, w_node_in, w_node_out, cot_nodes, cot_edges
):
    padded, ids, slot, sel, pre_self = deliver(h_in[0], new_index, source, edge_in[0], w_edge_in)
    edge_new, node_new, grad_edge, ng, halo, hid, post, pre, summed, nhid, npre, npost, recv, send = layer(
        padded, source, sel, pre_self, edge_in[0], cot_nodes[0], cot_edges[0], w_edge_in, w_edge_out, w_node_in, w_node_out
    )
    back, fin = collect(
        ng, halo, ids, edge_in[0], padded, hid, post, pre, summed, nhid, npre, npost, recv, send
    )
    grad_in, weight_grads = finish(back, slot, fin)
    return (node_new[None], edge_new[None], grad_in[None], grad_edge[None], weight_grads)


def solution(mesh):
    return jax.shard_map(
        local,
        mesh=mesh,
        in_specs=(
            P("geom", "dom", None),
            P("geom", "dom", None),
            P("geom", "dom"),
            P("geom", "dom"),
            P(),
            P(),
            P(),
            P(),
            P("geom", "dom", None),
            P("geom", "dom", None),
        ),
        out_specs=(
            P("geom", "dom", None),
            P("geom", "dom", None),
            P("geom", "dom", None),
            P("geom", "dom", None),
            P("dom", None),
        ),
        check_vma=False,
    )
```

```python
import functools
import math

import jax
import jax.numpy as jnp
from jax import lax
from jax.experimental import pallas as pl
from jax.experimental.pallas import tpu as pltpu
from jax.sharding import PartitionSpec as P

MESH = pl.DeviceIdType.MESH
BF = jnp.bfloat16
F32 = jnp.float32

D = 512
K = 4
C = 512
HB = 64
PADDED = C + 2 * HB
NP = 16
CAP = 48
SLOTS = NP * CAP
TC = 256
TE = TC * K
TILES = C // TC
SEL = PADDED + TC
RC = 64
SQUARES = 7
PER_DOM = SQUARES * D // NP


def nn(a, b):
    return jnp.dot(a, b, preferred_element_type=F32)


def nt(a, b):
    return lax.dot_general(a, b, (((1,), (1,)), ((), ())), preferred_element_type=F32)


def tn(a, b):
    return lax.dot_general(a, b, (((0,), (0,)), ((), ())), preferred_element_type=F32)


def sigmoid(v):
    return 0.5 * jnp.tanh(0.5 * v) + 0.5


def iota(shape, dim):
    return lax.broadcasted_iota(jnp.int32, shape, dim)


def remote(src, dst, send, recv, geom, dom):
    return pltpu.make_async_remote_copy(
        src_ref=src,
        dst_ref=dst,
        send_sem=send,
        recv_sem=recv,
        device_id=(geom, dom),
        device_id_type=MESH,
    )


def signal(sem, geom, dom):
    pl.semaphore_signal(sem, inc=1, device_id=(geom, dom), device_id_type=MESH)


def pack_matrix(slot):
    return (iota((SLOTS, C), 0) == slot).astype(BF)


def unpack_blocks(ids):
    turned = ids.T
    lanes = iota((CAP, C), 1).astype(F32)
    return [(turned[0:CAP, p : p + 1] == lanes).astype(BF) for p in range(NP)]


def deliver_kernel(
    h_hbm, tgt_hbm, src_hbm, edges_hbm, w_hbm,
    pad_ref, ids_ref, slot_ref, sel_ref, self_ref,
    h_ref, tgt_ref, src_ref, edges, w_self, sbuf, rbuf, sids, rids, edge_out, edge_in, mt,
    send, recv, isend, irecv, hsend, hrecv, lsem,
):
    geom = lax.axis_index("geom")
    me = lax.axis_index("dom")
    barrier = pltpu.get_barrier_semaphore()
    for p in range(1, NP):
        signal(barrier, geom, (me + p) % NP)

    loads = [
        pltpu.make_async_copy(far, near, lsem.at[n])
        for n, (far, near) in enumerate(
            ((tgt_hbm, tgt_ref), (h_hbm, h_ref), (edges_hbm, edges), (w_hbm.at[0:D], w_self), (src_hbm, src_ref))
        )
    ]
    for load in loads:
        load.start()
    loads[0].wait()
    tgt = tgt_ref[...]
    off = ((tgt >> 9) - me) & (NP - 1)
    row = tgt & (C - 1)
    owned = (iota((NP, C), 0) == off).astype(F32)
    upper = (iota((C, C), 0) < iota((C, C), 1)).astype(BF)
    before = nn(owned.astype(BF), upper)
    rank = jnp.sum(owned * before, axis=0, keepdims=True).astype(jnp.int32)
    slot = off * CAP + rank
    slot_ref[...] = slot
    ranked = (iota((128, C), 0) == rank).astype(BF)
    high = (row >> 5).astype(F32)
    low = (row & 31).astype(F32)
    coded = nt(jnp.concatenate([owned * high, owned * low, owned], axis=0).astype(BF), ranked)
    ids = 32.0 * coded[0:NP] + coded[NP : 2 * NP] + coded[2 * NP :] - 1.0
    for p in range(NP):
        sids[p] = jnp.broadcast_to(ids[p : p + 1, :], (8, 128))
    loads[1].wait()
    packed = nn(pack_matrix(slot), h_ref[...]).astype(BF)
    sbuf[...] = packed.reshape(NP, CAP, D)
    rbuf[0] = packed[0:CAP]

    pl.semaphore_wait(barrier, NP - 1)
    copies = []
    for p in range(1, NP):
        peer = (me + p) % NP
        copies.append(remote(sids.at[p], rids.at[p], isend.at[p], irecv.at[p], geom, peer))
        copies.append(remote(sbuf.at[p], rbuf.at[p], send.at[p], recv.at[p], geom, peer))
    for copy in copies:
        copy.start()
    for load in loads[2:]:
        load.wait()
    for t in range(TILES):
        rows = slice(t * TE, (t + 1) * TE)
        src = src_ref[:, rows] - (me * C - HB)
        src_col = jnp.broadcast_to(src.astype(F32), (128, TE)).T.astype(jnp.int32)
        for b in range(PADDED // 128):
            sel_ref[rows, b * 128 : (b + 1) * 128] = (src_col == iota((TE, 128), 1) + b * 128).astype(BF)
        self_ref[rows, :] = nn(edges[rows, :], w_self[...]).astype(BF)
    for copy in copies[0::2]:
        copy.wait_recv()
    got = jnp.concatenate([ids[0:1]] + [rids[p, 0:1, :] for p in range(1, NP)], axis=0)
    ids_ref[...] = got
    for p, block in enumerate(unpack_blocks(got)):
        mt[pl.ds(p * CAP, CAP), :] = block
    for copy in copies[1::2]:
        copy.wait_recv()
    arrived = rbuf[...].reshape(SLOTS, D)
    first = tn(mt[:, 0:128], arrived).astype(BF)
    last = tn(mt[:, C - 128 : C], arrived).astype(BF)
    edge_out[0] = first[0:HB]
    edge_out[1] = last[128 - HB : 128]
    to_prev = remote(edge_out.at[0], edge_in.at[1], hsend.at[0], hrecv.at[1], geom, (me + NP - 1) % NP)
    to_next = remote(edge_out.at[1], edge_in.at[0], hsend.at[1], hrecv.at[0], geom, (me + 1) % NP)
    to_prev.start()
    to_next.start()
    pad_ref[HB : HB + 128, :] = first
    pad_ref[HB + C - 128 : HB + C, :] = last
    pad_ref[HB + 128 : HB + C - 128, :] = tn(mt[:, 128 : C - 128], arrived).astype(BF)
    to_prev.wait_recv()
    to_next.wait_recv()
    pad_ref[0:HB, :] = edge_in[0]
    pad_ref[HB + C :, :] = edge_in[1]
    for copy in copies:
        copy.wait_send()
    to_prev.wait_send()
    to_next.wait_send()


def deliver(h, tgt, source, edges, wei):
    vm = pl.BlockSpec(memory_space=pltpu.VMEM)
    hbm = pl.BlockSpec(memory_space=pltpu.HBM)
    return pl.pallas_call(
        deliver_kernel,
        out_shape=(
            jax.ShapeDtypeStruct((PADDED, D), BF),
            jax.ShapeDtypeStruct((NP, 128), F32),
            jax.ShapeDtypeStruct((1, C), jnp.int32),
            jax.ShapeDtypeStruct((C * K, PADDED), BF),
            jax.ShapeDtypeStruct((C * K, D), BF),
        ),
        in_specs=[hbm] * 5,
        out_specs=(vm,) * 5,
        scratch_shapes=[
            pltpu.VMEM((C, D), BF),
            pltpu.VMEM((1, C), jnp.int32),
            pltpu.VMEM((1, C * K), jnp.int32),
            pltpu.VMEM((C * K, D), BF),
            pltpu.VMEM((D, D), BF),
            pltpu.VMEM((NP, CAP, D), BF),
            pltpu.VMEM((NP, CAP, D), BF),
            pltpu.VMEM((NP, 8, 128), F32),
            pltpu.VMEM((NP, 8, 128), F32),
            pltpu.VMEM((2, HB, D), BF),
            pltpu.VMEM((2, HB, D), BF),
            pltpu.VMEM((SLOTS, C), BF),
        ]
        + [pltpu.SemaphoreType.DMA((NP,))] * 4
        + [pltpu.SemaphoreType.DMA((2,))] * 2
        + [pltpu.SemaphoreType.DMA((5,))],
        compiler_params=pltpu.CompilerParams(
            collective_id=0, has_side_effects=True, vmem_limit_bytes=18 * 1024 * 1024
        ),
        cost_estimate=pl.CostEstimate(flops=20_000_000_000, bytes_accessed=60_000_000, transcendentals=0),
        name="deliver",
    )(*(pltpu.with_memory_space_constraint(a, pltpu.HBM) for a in (h, tgt, source, edges, wei)))


def layer_kernel(
    pad_ref, src_all, sel_all, self_all, edges_all, cotn_all, cote_all, wei_ref, weo_ref, wni_ref, wno_ref,
    edge_new_ref, node_new_ref, grad_edge_ref, ng_ref, halo_ref,
    hid_all, post_all, pre_all, summed_all, node_hid_all, node_pre_all, node_post_all, recv_all, send_ref,
    spread, four, comb, big, slope, normed, inv, ups, total,
):
    step = pl.program_id(0)
    me = lax.axis_index("dom")
    w_self, w_send, w_recv = wei_ref.at[0:D], wei_ref.at[D : 2 * D], wei_ref.at[2 * D : 3 * D]
    w_nself, w_nagg = wni_ref.at[0:D], wni_ref.at[D : 2 * D]
    rows = pl.ds(pl.multiple_of(step * TC, TC), TC)
    lines = pl.ds(pl.multiple_of(step * TE, TE), TE)
    sel_ref, self_ref, edges_ref, cote_ref = (ref.at[lines] for ref in (sel_all, self_all, edges_all, cote_all))
    hid, post_grad, pre_grad = (ref.at[lines] for ref in (hid_all, post_all, pre_all))
    cotn_ref, summed_ref, node_hid_ref, node_pre_ref, node_post_ref, recv_ref = (
        ref.at[rows] for ref in (cotn_all, summed_all, node_hid_all, node_pre_all, node_post_all, recv_all)
    )

    @pl.when(step == 0)
    def _():
        comb[0:PADDED, :] = nn(pad_ref[...], w_send[...]).astype(BF)
        spread[...] = (iota((TE, TC), 0) // K == iota((TE, TC), 1)).astype(BF)
        four[...] = (iota((TC, TE), 1) // K == iota((TC, TE), 0)).astype(BF)
        total[...] = jnp.zeros_like(total)

    nodes = pad_ref[pl.ds(pl.multiple_of(HB + step * TC, HB), TC), :]
    comb[PADDED:, :] = nn(nodes, w_recv[...]).astype(BF)

    big[...] = self_ref[...].astype(F32) + nn(jnp.concatenate([sel_ref[...], spread[...]], axis=1), comb[...])
    for r in range(0, TE, RC):
        v = big[r : r + RC, :]
        s = sigmoid(v)
        h = v * s
        hid[r : r + RC, :] = h.astype(BF)
        slope[r : r + RC, :] = s + h * (1.0 - s)
    big[...] = nn(hid[...], weo_ref[...])
    for r in range(0, TE, RC):
        v = big[r : r + RC, :]
        center = v - jnp.mean(v, axis=-1, keepdims=True)
        i = lax.rsqrt(jnp.mean(center * center, axis=-1, keepdims=True) + 1e-05)
        n = center * i
        normed[r : r + RC, :] = n
        inv[r : r + RC, :] = jnp.broadcast_to(i, (RC, 128))
        edge_new_ref[r : r + RC, :] = (edges_ref[r : r + RC, :].astype(F32) + n).astype(BF)

    summed = nn(four[...], edge_new_ref[...]).astype(BF)
    summed_ref[...] = summed
    v = nn(jnp.concatenate([nodes, summed], axis=1), wni_ref[...])
    s = sigmoid(v)
    h = v * s
    node_slope = s + h * (1.0 - s)
    node_hid = h.astype(BF)
    node_hid_ref[...] = node_hid
    v = nn(node_hid, wno_ref[...])
    center = v - jnp.mean(v, axis=-1, keepdims=True)
    i = lax.rsqrt(jnp.mean(center * center, axis=-1, keepdims=True) + 1e-05)
    n = center * i
    node_new_ref[...] = (nodes.astype(F32) + n).astype(BF)
    u = cotn_ref[...].astype(F32)
    m1 = jnp.mean(u, axis=-1, keepdims=True)
    m2 = jnp.mean(u * n, axis=-1, keepdims=True)
    node_post_grad = (i * (u - m1 - n * m2)).astype(BF)
    node_post_ref[...] = node_post_grad
    node_pre_grad = (nt(node_post_grad, wno_ref[...]) * node_slope).astype(BF)
    node_pre_ref[...] = node_pre_grad
    spread_grad = nt(node_pre_grad, w_nagg[...]).astype(BF)

    ups[...] = nn(spread[...], spread_grad)
    for r in range(0, TE, RC):
        u = cote_ref[r : r + RC, :].astype(F32) + ups[r : r + RC, :]
        ups[r : r + RC, :] = u
        n = normed[r : r + RC, :]
        m1 = jnp.mean(u, axis=-1, keepdims=True)
        m2 = jnp.mean(u * n, axis=-1, keepdims=True)
        post_grad[r : r + RC, :] = (inv[r : r + RC, 0:1] * (u - m1 - n * m2)).astype(BF)
    big[...] = nt(post_grad[...], weo_ref[...])
    for r in range(0, TE, RC):
        pre_grad[r : r + RC, :] = (big[r : r + RC, :] * slope[r : r + RC, :]).astype(BF)
    g = pre_grad[...]
    big[...] = nt(g, w_self[...])
    for r in range(0, TE, RC):
        grad_edge_ref[r : r + RC, :] = (ups[r : r + RC, :] + big[r : r + RC, :]).astype(BF)
    src = src_all[:, lines] - (me * C - HB)
    sel_t = (iota((PADDED, TE), 0) == src).astype(BF)
    gathered = nn(jnp.concatenate([sel_t, four[...]], axis=0), g)
    total[...] += gathered[0:PADDED]
    recv_grad = gathered[PADDED:].astype(BF)
    recv_ref[...] = recv_grad
    ng_ref[rows, :] = (
        cotn_ref[...].astype(F32) + nt(node_pre_grad, w_nself[...]) + nt(recv_grad, w_recv[...])
    )

    @pl.when(step == TILES - 1)
    def _():
        t = total[...].astype(BF)
        send_ref[...] = t
        back = nt(t, w_send[...])
        ng_ref[...] += back[HB : HB + C]
        halo_ref[0] = back[0:HB].astype(BF)
        halo_ref[1] = back[HB + C :].astype(BF)


def layer(padded, source, sel, pre_self, edges, cot_nodes, cot_edges, wei, weo, wni, wno):
    vm = pl.BlockSpec(memory_space=pltpu.VMEM)

    def tile(rows):
        return pl.BlockSpec((rows, D), lambda i: (i, 0))

    by_edge = jax.ShapeDtypeStruct((C * K, D), BF)
    by_cell = jax.ShapeDtypeStruct((C, D), BF)
    return pl.pallas_call(
        layer_kernel,
        grid=(TILES,),
        out_shape=(
            by_edge, by_cell, by_edge,
            jax.ShapeDtypeStruct((C, D), F32),
            jax.ShapeDtypeStruct((2, HB, D), BF),
            by_edge, by_edge, by_edge, by_cell, by_cell, by_cell, by_cell, by_cell,
            jax.ShapeDtypeStruct((PADDED, D), BF),
        ),
        in_specs=[vm] * 11,
        out_specs=(tile(TE), tile(TC), tile(TE)) + (vm,) * 11,
        scratch_shapes=[
            pltpu.VMEM((TE, TC), BF),
            pltpu.VMEM((TC, TE), BF),
            pltpu.VMEM((SEL, D), BF),
            pltpu.VMEM((TE, D), F32),
            pltpu.VMEM((TE, D), F32),
            pltpu.VMEM((TE, D), F32),
            pltpu.VMEM((TE, 128), F32),
            pltpu.VMEM((TE, D), F32),
            pltpu.VMEM((PADDED, D), F32),
        ],
        compiler_params=pltpu.CompilerParams(vmem_limit_bytes=30 * 1024 * 1024),
        cost_estimate=pl.CostEstimate(flops=20_000_000_000, bytes_accessed=40_000_000, transcendentals=4_000_000),
        name="layer",
    )(padded, source, sel, pre_self, edges, cot_nodes, cot_edges, wei, weo, wni, wno)


ROWS = SQUARES * D
QW = 128
CW = 2 * QW
EARLY = 10
PART = 64
STARTS = (0, 64, 128, 160)


def collect_kernel(
    ng_ref, halo_ref, ids_ref,
    edges, pad, hid, post, pre, summed, nhid, npre, npost, recv_g, send_g,
    back_ref, fin_ref,
    hbuf, sback, rback, wown, wsend, pbuf, wsum, r1, p1, r2, r3, fin, wx, rx, px, ri, ag,
    hsend, hrecv, bsend, brecv, psend, precv, s1, v1, s2, v2, s3, v3, s4, v4, sx, vx, si, vi, sg, vg,
):
    geom = lax.axis_index("geom")
    me = lax.axis_index("dom")
    core = geom % 2
    x = geom // 2
    y = me // 4
    z = me % 4
    partner = x * 2 + (1 - core)
    i_me = y * (1 - core) + z * core
    j_me = z * (1 - core) + y * core

    def dom_of(i, j):
        return (i * 4 + j) * (1 - core) + (j * 4 + i) * core

    barrier = pltpu.get_barrier_semaphore()
    signals = NP - 1
    for p in range(1, NP):
        signal(barrier, geom, (me + p) % NP)
    for d in range(1, 8):
        signal(barrier, (geom + d) % 8, me)
        signals += 1

    scale = 1.0 / math.sqrt(8 * NP * C * K)
    inner = slice(HB, HB + C)
    operands = {
        0: (edges, None, pre), 1: (pad, None, send_g), 2: (pad, inner, recv_g), 3: (hid, None, post),
        4: (pad, inner, npre), 5: (summed, None, npre), 6: (nhid, None, npost),
    }
    pair = {}

    def square(q):
        left, cut, right = operands[q]
        rows = left[...] if cut is None else left[cut, :]
        value = (tn(rows, right[...]) * scale).astype(BF)
        for c in range(2):
            low, high = value[:, c * CW : c * CW + QW], value[:, c * CW + QW : (c + 1) * CW]
            wown[c, q] = jnp.where(core == 0, low, high)
            wsend[c, q] = jnp.where(core == 0, high, low)
            n = c * SQUARES + q
            pair[c, q] = remote(wsend.at[c, q], pbuf.at[c, q], psend.at[n], precv.at[n], partner, me)

    def reduced_block(c, k):
        parts = []
        at, end = k * PER_DOM, (k + 1) * PER_DOM
        while at < end:
            q, r = divmod(at, D)
            n = min(end - at, D - r)
            parts.append(wown[c, q, r : r + n].astype(F32) + pbuf[c, q, r : r + n].astype(F32))
            at += n
        value = parts[0] if len(parts) == 1 else jnp.concatenate(parts, axis=0)
        return value.astype(BF)

    seen = set()

    def joined(c, squares):
        for q in squares:
            if (c, q) not in seen:
                seen.add((c, q))
                pair[c, q].wait_recv()

    ones, xs, ys = {}, [], []

    def join(c):
        joined(c, range(SQUARES))
        for k in range(NP):
            i = (k // 4) * (1 - core) + (k % 4) * core
            j = (k % 4) * (1 - core) + (k // 4) * core
            wsum[pl.ds(i * 4 + j, 1)] = reduced_block(c, k).reshape(1, PER_DOM, QW)
        for d in range(1, 4):
            to = (i_me + d) % 4
            ones[d] = remote(
                wsum.at[pl.ds(to * 4, 4)], r1.at[d - 1], s1.at[d - 1], v1.at[d - 1], geom, dom_of(to, j_me)
            )
            ones[d].start()

    def join_x(c, low, high, squares):
        joined(c, squares)
        for k in range(low, high):
            value = reduced_block(c, k)
            for n, r in enumerate(STARTS):
                wx[n, k] = value[r : r + PART]
        for d in range(1, 4):
            to = (x + d) % 4
            n = len(xs)
            xs.append(
                remote(
                    wx.at[to, low:high], rx.at[d - 1, low:high], sx.at[n], vx.at[n], to * 2 + core, me
                )
            )
            xs[-1].start()

    def narrow_x():
        for copy in xs:
            copy.wait_recv()
        own = wx[pl.ds(x, 1)].reshape(NP, PART, QW).astype(F32)
        for d in range(3):
            own += rx[d].astype(F32)
        px[...] = own.astype(BF)
        for d in range(1, NP):
            to = (me + d) % NP
            ys.append(remote(px.at[to], ri.at[d - 1], si.at[d - 1], vi.at[d - 1], geom, to))
            ys[-1].start()

    gathers = []

    def narrow_dom():
        for copy in ys:
            copy.wait_recv()
        own = px[pl.ds(me, 1)].reshape(PART, QW).astype(F32)
        for d in range(NP - 1):
            own += ri[d].astype(F32)
        ag[pl.ds(geom, 1)] = own.astype(BF).reshape(1, PART, QW)
        for d in range(1, 8):
            gathers.append(
                remote(ag.at[geom], ag.at[geom], sg.at[d - 1], vg.at[d - 1], (geom + d) % 8, me)
            )
            gathers[-1].start()

    twos, threes = {}, {}

    def narrow():
        for d in range(1, 4):
            ones[d].wait_recv()
        for j in range(4):
            own = wsum[pl.ds(i_me * 4 + j, 1)].reshape(PER_DOM, QW).astype(F32)
            for d in range(3):
                own += r1[d, j].astype(F32)
            p1[j] = own.astype(BF)
        for d in range(1, 4):
            j = (j_me + d) % 4
            twos[d] = remote(p1.at[j], r2.at[d - 1], s2.at[d - 1], v2.at[d - 1], geom, dom_of(i_me, j))
            twos[d].start()

    def across():
        for d in range(1, 4):
            twos[d].wait_recv()
        own = p1[pl.ds(j_me, 1)].reshape(PER_DOM, QW).astype(F32)
        for d in range(3):
            own += r2[d].astype(F32)
        r3[pl.ds(x, 1)] = own.astype(BF).reshape(1, PER_DOM, QW)
        for d in range(1, 4):
            threes[d] = remote(r3.at[x], r3.at[x], s3.at[d - 1], v3.at[d - 1], ((x + d) % 4) * 2 + core, me)
            threes[d].start()

    def send_pairs(*squares):
        for c in (1, 0):
            for q in squares:
                pair[c, q].start()

    for q in (4, 5, 6, 3, 2, 1, 0):
        square(q)
    pl.semaphore_wait(barrier, signals)
    send_pairs(4, 5, 6)
    to_prev = remote(halo_ref.at[0], hbuf.at[1], hsend.at[0], hrecv.at[1], geom, (me + NP - 1) % NP)
    to_next = remote(halo_ref.at[1], hbuf.at[0], hsend.at[1], hrecv.at[0], geom, (me + 1) % NP)
    to_prev.start()
    to_next.start()
    send_pairs(3, 2, 1, 0)
    join_x(1, EARLY, NP, (4, 5, 6))
    join_x(1, 0, EARLY, range(SQUARES))
    join(0)

    blocks = jnp.concatenate(unpack_blocks(ids_ref[...]), axis=0)
    to_prev.wait_recv()
    to_next.wait_recv()
    first = ng_ref[0:HB, :] + hbuf[0].astype(F32)
    last = ng_ref[C - HB :, :] + hbuf[1].astype(F32)
    cells = jnp.concatenate([first, ng_ref[HB : C - HB, :], last], axis=0).astype(BF)
    packed = nn(blocks, cells).astype(BF)
    sback[...] = packed.reshape(NP, CAP, D)
    rback[0] = packed[0:CAP]
    backs = [
        remote(sback.at[p], rback.at[p], bsend.at[p], brecv.at[p], geom, (me + NP - p) % NP)
        for p in range(1, NP)
    ]
    for copy in backs:
        copy.start()

    narrow()
    narrow_x()
    across()
    narrow_dom()
    for copy in backs:
        copy.wait_recv()
    back_ref[...] = rback[...].reshape(SLOTS, D)
    for d in range(1, 4):
        origin = (x + 4 - d) % 4
        remote(r3.at[x], r3.at[origin], s3.at[d - 1], v3.at[d - 1], origin * 2 + core, me).wait_recv()
    done = r3[0].astype(F32) + r3[1].astype(F32) + r3[2].astype(F32) + r3[3].astype(F32)
    fin[pl.ds(core, 1)] = done.astype(BF).reshape(1, PER_DOM, QW)
    four = remote(fin.at[core], fin.at[core], s4, v4, partner, me)
    four.start()
    for d in range(1, 8):
        origin = (geom + 8 - d) % 8
        remote(ag.at[geom], ag.at[origin], sg.at[d - 1], vg.at[d - 1], origin, me).wait_recv()
    for q in range(2):
        for n, r in enumerate(STARTS):
            fin_ref[r : r + PART, CW + q * QW : CW + (q + 1) * QW] = ag[n * 2 + q]
    remote(fin.at[core], fin.at[1 - core], s4, v4, partner, me).wait_recv()
    for q in range(2):
        fin_ref[:, q * QW : (q + 1) * QW] = fin[q]
    groups = (pair, ones, twos, threes)
    for copy in [to_prev, to_next, four] + backs + xs + ys + gathers:
        copy.wait_send()
    for group in groups:
        for copy in group.values():
            copy.wait_send()


def finish_kernel(back_ref, slot_ref, fin_ref, grad_ref, out_ref):
    grad_ref[...] = tn(pack_matrix(slot_ref[...]), back_ref[...]).astype(BF)
    out_ref[...] = fin_ref[...].astype(F32)


def finish(back, slot, fin):
    vm = pl.BlockSpec(memory_space=pltpu.VMEM)
    return pl.pallas_call(
        finish_kernel,
        out_shape=(jax.ShapeDtypeStruct((C, D), BF), jax.ShapeDtypeStruct((PER_DOM, D), F32)),
        in_specs=[vm] * 3,
        out_specs=(vm, vm),
        compiler_params=pltpu.CompilerParams(vmem_limit_bytes=8 * 1024 * 1024),
        name="finish",
    )(back, slot, fin)


def collect(ng, halo, ids, *operands):
    vm = pl.BlockSpec(memory_space=pltpu.VMEM)
    dma = pltpu.SemaphoreType.DMA
    return pl.pallas_call(
        collect_kernel,
        out_shape=(
            jax.ShapeDtypeStruct((SLOTS, D), BF),
            jax.ShapeDtypeStruct((PER_DOM, D), BF),
        ),
        in_specs=[vm] * (3 + len(operands)),
        out_specs=(vm, vm),
        scratch_shapes=[
            pltpu.VMEM((2, HB, D), BF),
            pltpu.VMEM((NP, CAP, D), BF),
            pltpu.VMEM((NP, CAP, D), BF),
            pltpu.VMEM((2, SQUARES, D, QW), BF),
            pltpu.VMEM((2, SQUARES, D, QW), BF),
            pltpu.VMEM((2, SQUARES, D, QW), BF),
            pltpu.VMEM((NP, PER_DOM, QW), BF),
            pltpu.VMEM((3, 4, PER_DOM, QW), BF),
            pltpu.VMEM((4, PER_DOM, QW), BF),
            pltpu.VMEM((3, PER_DOM, QW), BF),
            pltpu.VMEM((4, PER_DOM, QW), BF),
            pltpu.VMEM((2, PER_DOM, QW), BF),
            pltpu.VMEM((4, NP, PART, QW), BF),
            pltpu.VMEM((3, NP, PART, QW), BF),
            pltpu.VMEM((NP, PART, QW), BF),
            pltpu.VMEM((NP - 1, PART, QW), BF),
            pltpu.VMEM((8, PART, QW), BF),
            dma((2,)), dma((2,)), dma((NP,)), dma((NP,)),
            dma((2 * SQUARES,)), dma((2 * SQUARES,)), dma((3,)), dma((3,)),
            dma((3,)), dma((3,)), dma((3,)), dma((3,)), dma, dma,
            dma((6,)), dma((6,)), dma((NP - 1,)), dma((NP - 1,)), dma((7,)), dma((7,)),
        ],
        compiler_params=pltpu.CompilerParams(
            collective_id=1, has_side_effects=True, vmem_limit_bytes=32 * 1024 * 1024
        ),
        name="collect",
    )(ng, halo, ids, *operands)


def local(
    h_in, edge_in, new_index, source, w_edge_in, w_edge_out, w_node_in, w_node_out, cot_nodes, cot_edges
):
    padded, ids, slot, sel, pre_self = deliver(h_in[0], new_index, source, edge_in[0], w_edge_in)
    edge_new, node_new, grad_edge, ng, halo, hid, post, pre, summed, nhid, npre, npost, recv, send = layer(
        padded, source, sel, pre_self, edge_in[0], cot_nodes[0], cot_edges[0], w_edge_in, w_edge_out, w_node_in, w_node_out
    )
    back, fin = collect(
        ng, halo, ids, edge_in[0], padded, hid, post, pre, summed, nhid, npre, npost, recv, send
    )
    grad_in, weight_grads = finish(back, slot, fin)
    return (node_new[None], edge_new[None], grad_in[None], grad_edge[None], weight_grads)


def solution(mesh):
    return jax.shard_map(
        local,
        mesh=mesh,
        in_specs=(
            P("geom", "dom", None),
            P("geom", "dom", None),
            P("geom", "dom"),
            P("geom", "dom"),
            P(),
            P(),
            P(),
            P(),
            P("geom", "dom", None),
            P("geom", "dom", None),
        ),
        out_specs=(
            P("geom", "dom", None),
            P("geom", "dom", None),
            P("geom", "dom", None),
            P("geom", "dom", None),
            P("dom", None),
        ),
        check_vma=False,
    )
```
